32 devices in a mesh: mp: 4 (over x, core), seq: 8 (over z, y).
Axes of the slice: x: 2, y: 2, z: 4, core: 2. Of those that a mesh axis runs over, the one named last changes fastest.
Arguments:
- hidden_in: bfloat16 [2048, 5376], P('seq', 'mp'), may hold values from -28 to 28
- gain_in: float32 [5376], replicated, may hold values from 0.3 to 3
- w_query: bfloat16 [5376, 4096], P('seq', 'mp'), may hold values from -0.078125 to 0.078125
- key_weight: bfloat16 [5376, 2048], P('seq', 'mp'), may hold values from -0.078125 to 0.078125
- value_weight: bfloat16 [5376, 2048], P('seq', 'mp'), may hold values from -0.078125 to 0.078125
- gain_query: float32 [128], replicated, may hold values from 0.3 to 3
- gain_key: float32 [128], replicated, may hold values from 0.3 to 3
- start_pos: int32 [1], replicated, may hold values from 1024 to 4095
- cached_key_rows: bfloat16 [1024, 2048], P(None, 'mp'), may hold values from -140 to 140
- cached_value_rows: bfloat16 [1024, 2048], P(None, 'mp'), may hold values from -5 to 5
- w_out: bfloat16 [4096, 5376], P('seq', 'mp'), may hold values from -1.5 to 1.5
- gain_post: float32 [5376], P('mp'), may hold values from 0.3 to 3
Outputs:
- hidden_out: bfloat16 [2048, 5376], P('seq', 'mp')
The draws below stay inside these ranges and needn't reach their ends.
All inputs are finite; a program needn't handle non-finite values.
Results may differ from the reference program's by a relative error of at most 0.012.
The reference program's roundings to bfloat16 on the way count: a program that leaves them out, or rounds other values in their place, can miss the bound.
Values may be sent and summed in bfloat16 or wider, within the bound.
A program may use at most 128 MiB of HBM per device.

```python
import math
import jax
import jax.numpy as jnp
from jax import lax

MODEL_WIDTH = 5376
QUERY_HEAD_COUNT = 32
KEY_VALUE_HEADS = 16
HEAD_SIZE = 128
WINDOW_LENGTH = 1024
STRETCH_TOKENS = 2048


def draw_hidden_in(key, part):
    streams = jax.random.split(key, 3)
    low = math.log(0.3)
    high = math.log(3.0)
    row_scale = jnp.exp(jax.random.uniform(streams[0], (STRETCH_TOKENS, 1), jnp.float32, low, high))
    col_scale = jnp.exp(jax.random.uniform(streams[1], (1, MODEL_WIDTH), jnp.float32, low, high))
    base = jax.random.truncated_normal(streams[2], -3.0, 3.0, (STRETCH_TOKENS, MODEL_WIDTH), jnp.float32)
    return (base * row_scale * col_scale).astype(jnp.bfloat16)


def draw_w_out(key, part):
    streams = jax.random.split(key, 2)
    fan_rows = QUERY_HEAD_COUNT * HEAD_SIZE
    col_scale = jnp.exp(jax.random.uniform(streams[0], (1, MODEL_WIDTH), jnp.float32, 0.0, math.log(10.0)))
    col_scale = col_scale * 3.0 ** (jnp.arange(MODEL_WIDTH, dtype=jnp.float32)[None, :] / MODEL_WIDTH)
    base = jax.random.truncated_normal(streams[1], -3.0, 3.0, (fan_rows, MODEL_WIDTH), jnp.float32)
    return jnp.clip(base * fan_rows ** (-0.5) * col_scale, -1.5, 1.5).astype(jnp.bfloat16)


def draw_cached_key_rows(key, part):
    streams = jax.random.split(key, 1)
    column_range = KEY_VALUE_HEADS * HEAD_SIZE
    base = jax.random.truncated_normal(streams[0], -4.0, 4.0, (WINDOW_LENGTH, column_range), jnp.float32)
    return base.astype(jnp.bfloat16)


def block_scale(rng, shape, cuts, low, largest):
    level, own = 1.0, jax.random.fold_in(rng, 6)
    for position, shards_of in cuts:
        steps = jnp.exp(jax.random.uniform(jax.random.fold_in(own, position), (shards_of,), jnp.float32, low / len(cuts), largest / len(cuts)))
        level = level * jnp.repeat(steps, shape[position] // shards_of).reshape([-1 if axis == position else 1 for axis in range(len(shape))])
    return level


def bell_draw(stream_key, extent, width, most, cuts=(), kind=jnp.bfloat16):
    entries = jax.random.normal(stream_key, extent, jnp.float32) * width
    if len(cuts) > 0:
        entries = block_scale(stream_key, extent, cuts, -0.22, 0.18) * entries
    return jnp.clip(entries, min=-most, max=most).astype(kind)


def setup_inputs(seed: int = 0) -> dict:
    seeds = jax.random.split(jax.random.key(seed), 13)
    return {
        "hidden_in": draw_hidden_in(jax.random.fold_in(seeds[12], 71), 0),
        "gain_in": jnp.clip(jnp.exp(jax.random.uniform(seeds[1], (MODEL_WIDTH,), jnp.float32, math.log(0.3), math.log(3.0))), 0.3, 3.0),
        "w_query": bell_draw(seeds[2], (MODEL_WIDTH, QUERY_HEAD_COUNT * HEAD_SIZE), MODEL_WIDTH ** -0.5, 0.078125, ((0, 8), (1, 4))),
        "key_weight": bell_draw(seeds[3], (MODEL_WIDTH, KEY_VALUE_HEADS * HEAD_SIZE), MODEL_WIDTH ** -0.5, 0.078125, ((0, 8), (1, 4))),
        "value_weight": bell_draw(seeds[4], (MODEL_WIDTH, KEY_VALUE_HEADS * HEAD_SIZE), MODEL_WIDTH ** -0.5, 0.078125, ((0, 8), (1, 4))),
        "gain_query": jnp.clip(jnp.exp(jax.random.uniform(seeds[5], (HEAD_SIZE,), jnp.float32, math.log(0.3), math.log(3.0))), 0.3, 3.0),
        "gain_key": jnp.clip(jnp.exp(jax.random.uniform(seeds[6], (HEAD_SIZE,), jnp.float32, math.log(0.3), math.log(3.0))), 0.3, 3.0),
        "start_pos": jax.random.randint(seeds[7], (1,), WINDOW_LENGTH, 4 * WINDOW_LENGTH).astype(jnp.int32),
        "cached_key_rows": draw_cached_key_rows(jax.random.fold_in(seeds[12], 71), 0),
        "cached_value_rows": bell_draw(seeds[9], (WINDOW_LENGTH, KEY_VALUE_HEADS * HEAD_SIZE), 1.0, 5.0, ((1, 4),)),
        "w_out": draw_w_out(jax.random.fold_in(seeds[12], 71), 0),
        "gain_post": jnp.clip(jnp.exp(math.log(3.0) - 2.3025851 * jax.random.uniform(seeds[11], (MODEL_WIDTH,), jnp.float32) ** block_scale(seeds[11], (MODEL_WIDTH,), ((0, 4),), -0.2, 0.2)), 0.3, 3.0),
    }


epsilon = 1e-06
query_scale = 168.0 ** (-0.5)
rope_base = 10000.0

def norm_rows(values, gain):
    return values * lax.rsqrt(lax.optimization_barrier(jnp.mean(values * values, axis=-1, keepdims=True)) + epsilon) * gain

def rotate(tensor, positions):
    half_dim = tensor.shape[-1] // 2
    inverse_freq = rope_base ** (-(jnp.arange(half_dim, dtype=jnp.float32) * 2.0) / tensor.shape[-1])
    angles = positions.astype(jnp.float32)[:, None, None] * inverse_freq[None, None, :]
    cosine = jnp.cos(angles)
    sine = jnp.sin(angles)
    first = tensor[..., :half_dim]
    second = tensor[..., half_dim:]
    return jnp.concatenate([first * cosine - second * sine, second * cosine + first * sine], axis=-1)

def reference(hidden_in, gain_in, w_query, key_weight, value_weight, gain_query, gain_key, start_pos, cached_key_rows, cached_value_rows, w_out, gain_post):
    residual_in = hidden_in.astype(jnp.float32)
    normed_hidden = norm_rows(residual_in, gain_in).astype(jnp.bfloat16)
    query_matrix = jnp.dot(normed_hidden, w_query, preferred_element_type=jnp.float32).reshape(STRETCH_TOKENS, QUERY_HEAD_COUNT, HEAD_SIZE)
    stretch_keys = jnp.dot(normed_hidden, key_weight, preferred_element_type=jnp.float32).reshape(STRETCH_TOKENS, KEY_VALUE_HEADS, HEAD_SIZE)
    stretch_values = jnp.dot(normed_hidden, value_weight, preferred_element_type=jnp.float32).astype(jnp.bfloat16).reshape(STRETCH_TOKENS, KEY_VALUE_HEADS, HEAD_SIZE)
    positions = start_pos[0] + jnp.arange(STRETCH_TOKENS, dtype=jnp.int32)
    query_matrix = (rotate(norm_rows(query_matrix, gain_query), positions) * query_scale).astype(jnp.bfloat16)
    stretch_keys = rotate(norm_rows(stretch_keys, gain_key), positions).astype(jnp.bfloat16)
    joined_keys = jnp.concatenate([cached_key_rows.reshape(WINDOW_LENGTH, KEY_VALUE_HEADS, HEAD_SIZE), stretch_keys], axis=0)
    joined_values = jnp.concatenate([cached_value_rows.reshape(WINDOW_LENGTH, KEY_VALUE_HEADS, HEAD_SIZE), stretch_values], axis=0)
    query_group_count = QUERY_HEAD_COUNT // KEY_VALUE_HEADS
    block_list = STRETCH_TOKENS // WINDOW_LENGTH
    grouped_queries = query_matrix.reshape(block_list, WINDOW_LENGTH, KEY_VALUE_HEADS, query_group_count, HEAD_SIZE)

    def one_block(inputs):
        query_block, block_index = inputs
        key_block = lax.dynamic_slice_in_dim(joined_keys, block_index * WINDOW_LENGTH, 2 * WINDOW_LENGTH, 0)
        value_block = lax.dynamic_slice_in_dim(joined_values, block_index * WINDOW_LENGTH, 2 * WINDOW_LENGTH, 0)
        scores = jnp.einsum('tkgd,skd->kgts', query_block.astype(jnp.float32), key_block.astype(jnp.float32))
        query_index = jnp.arange(WINDOW_LENGTH, dtype=jnp.int32)[:, None]
        key_index = jnp.arange(2 * WINDOW_LENGTH, dtype=jnp.int32)[None, :]
        visible = (key_index > query_index) & (key_index <= query_index + WINDOW_LENGTH)
        scores = jnp.where(visible, scores, -jnp.inf)
        row_max = lax.optimization_barrier(jnp.max(scores, axis=-1, keepdims=True))
        probs = jnp.exp(scores - row_max)
        totals = lax.optimization_barrier(jnp.sum(probs, axis=-1))
        probs_b = probs.astype(jnp.bfloat16)
        summed = jnp.einsum('kgts,skd->tkgd', probs_b.astype(jnp.float32), value_block.astype(jnp.float32))
        summed = summed / jnp.transpose(totals, (2, 0, 1))[..., None]
        return summed.reshape(WINDOW_LENGTH, QUERY_HEAD_COUNT * HEAD_SIZE).astype(jnp.bfloat16)
    attn = lax.map(one_block, (grouped_queries, jnp.arange(block_list, dtype=jnp.int32))).reshape(STRETCH_TOKENS, QUERY_HEAD_COUNT * HEAD_SIZE)
    mixed = jnp.dot(attn, w_out, preferred_element_type=jnp.float32)
    return (residual_in + norm_rows(mixed, gain_post)).astype(jnp.bfloat16)
```

```python
import functools

import jax
import jax.numpy as jnp
from jax import lax
from jax.experimental import pallas as pl
from jax.experimental.pallas import tpu as pltpu
from jax.sharding import PartitionSpec as P

MODEL_WIDTH = 5376
WINDOW_LENGTH = 1024


epsilon = 1e-06
query_scale = 168.0 ** (-0.5)
rope_base = 10000.0

MESH = pl.DeviceIdType.MESH
f32 = jnp.float32
bf16 = jnp.bfloat16


SCHEDULE = (
    ("wc", 0, 0), ("wo", 1), ("xz", 0), ("xz", 1), ("wc", 0, 1), ("xs", 1, 0), ("wc", 2, 0), ("wc", 1, 1),
    ("wd", 0, 0), ("wc", 1, 0), ("wo", 0), ("wr", 0, 1), ("xc", 1), ("wd", 0, 1), ("wc", 2, 1), ("wr", 0, 0),
    ("xx", 0), ("wr", 2, 0), ("wy", 0, 0), ("xs", 1, 1), ("xx", 1), ("wd", 2, 0), ("wy", 1, 0), ("xs", 2, 0),
    ("wy", 3, 0), ("wr", 2, 1), ("wr", 1, 1), ("xk", 1, 0), ("wd", 2, 1), ("wy", 2, 0), ("wy", 0, 2),
    ("wd", 1, 1), ("wy", 0, 1), ("xc", 0), ("wy", 3, 2), ("xs", 2, 1), ("xk", 1, 1), ("nm", 1), ("we", 0),
    ("xk", 0, 0), ("xs", 3, 0), ("wr", 1, 0), ("xk", 2, 0), ("wy", 1, 2), ("wy", 2, 2), ("xk", 2, 1),
    ("xs", 3, 1), ("xk", 3, 0), ("ca", 0), ("xk", 0, 1), ("wd", 1, 0), ("wy", 1, 1), ("nm", 2), ("wy", 2, 1),
    ("wy", 3, 1), ("xk", 3, 1), ("nm", 0), ("nm", 3), ("we", 1), ("we", 2), ("we", 3),
)


def layer_kernel(
    hidden, gain_in, wq, wk, wv, gain_q, gain_k, cos_t, sin_t, cache_k, cache_v, wo, gain_post,
    out,
    xb, xn, tb, wb, ob, kv, qb, ab, rb, sb, ss, pacc,
    local_sem, xz_send, xz_recv, xx_send, xx_recv, xc_send, xc_recv,
    w_send, t_recv, rl_send, wz_recv, wy_send, wy_recv, c_send, c_recv, oy_send, oy_recv,
    kv_send, kv_recv, a_send, a_recv, r_send, r_recv, s_send, s_recv,
):
    NZ, NM = 4, 4
    rows, cols = hidden.shape
    depth = wq.shape[0]
    m = lax.axis_index("mp")
    s = lax.axis_index("seq")
    z, y = s // 2, s % 2
    x, c = m // 2, m % 2
    ypeer = {"mp": m, "seq": 2 * z + (1 - y)}
    xpeer_m = (1 - x) * 2 + c
    cpeer_m = x * 2 + (1 - c)
    xdiag_m = (1 - x) * 2 + (1 - c)
    xpeer = {"mp": xpeer_m, "seq": s}
    cpeer = {"mp": cpeer_m, "seq": s}

    def at_z(zz):
        return {"mp": m, "seq": 2 * zz + y}

    def remote(src, dst, send, recv, dev):
        return pltpu.make_async_remote_copy(
            src_ref=src, dst_ref=dst, send_sem=send, recv_sem=recv,
            device_id=dev, device_id_type=MESH)

    def pick(a0, a1, a2, a3):
        return jnp.where(z == 0, a0, jnp.where(z == 1, a1, jnp.where(z == 2, a2, a3)))

    near = [z, pick(1, 0, 1, 2), pick(2, 2, 3, 1), pick(3, 3, 0, 0)]

    barrier = pltpu.get_barrier_semaphore()
    for d in range(1, 4):
        pl.semaphore_signal(barrier, inc=1, device_id=at_z((z + d) % 4), device_id_type=MESH)
        pl.semaphore_signal(
            barrier, inc=1, device_id={"mp": cpeer_m, "seq": 2 * ((z + d) % 4) + y}, device_id_type=MESH)
        pl.semaphore_signal(barrier, inc=1, device_id={"mp": (m + d) % 4, "seq": s}, device_id_type=MESH)
    pl.semaphore_signal(barrier, inc=1, device_id=ypeer, device_id_type=MESH)

    spans = [(0, 256), (256, 128), (384, 128)]

    def w_src(j, i):
        width = spans[i][1]
        return (wq, wk, wv)[i].at[:, pl.ds(pl.multiple_of(j * width, 128), width)]

    def wb_at(zsrc, yy, i):
        return wb.at[zsrc, pl.ds(pl.multiple_of(yy * depth, 16), depth), pl.ds(*spans[i])]

    def tb_at(k, i):
        return tb.at[k, :, pl.ds(*spans[i])]

    def c_parts(j):
        return [
            (cache_k.at[:, pl.ds(j * 128, 128)], kv.at[pl.ds(0, 1024), pl.ds(0, 128)]),
            (cache_v.at[:, pl.ds(j * 128, 128)], kv.at[pl.ds(0, 1024), pl.ds(128, 128)]),
        ]

    own_x = pltpu.make_async_copy(hidden, xb.at[z, m], local_sem.at[0])
    own_w = [
        (m == z, pltpu.make_async_copy(w_src(m, i), wb_at(z, y, i), local_sem.at[1 + i])) for i in range(3)
    ]
    own_c = []
    for j in range(4):
        mine = (m == j) & (z == j)
        own_c.extend((mine, pltpu.make_async_copy(a, b, local_sem.at[4 + i])) for i, (a, b) in enumerate(c_parts(j)))
    own_o = [
        (None, pltpu.make_async_copy(wo.at[pl.ds(h * 256, 256), :], ob.at[2 * y + h], local_sem.at[6 + h]))
        for h in range(2)
    ]

    def when(cond, fn):
        if cond is None:
            fn()
        else:
            pl.when(cond)(fn)

    for cond, cp in [(None, own_x)] + own_w + own_c + own_o:
        when(cond, cp.start)

    pl.semaphore_wait(barrier, 10)

    pending = []

    def send(cond, cp):
        when(cond, cp.start)
        pending.append((cond, cp))

    half = rows // 2

    def xb_at(zz, mm, hf):
        return xb.at[zz, mm, pl.ds(hf * half, half), :]

    def x_src(zz, hf, own):
        return hidden.at[pl.ds(hf * half, half), :] if own else xb_at(zz, m, hf)

    def x_right(zz, hf, own=False):
        return remote(x_src(zz, hf, own), xb_at(zz, m, hf), xz_send.at[0, zz, hf], xz_recv.at[zz, hf], at_z((z + 1) % 4))

    def x_left(zz, hf, own=False):
        return remote(x_src(zz, hf, own), xb_at(zz, m, hf), xz_send.at[1, zz, hf], xz_recv.at[zz, hf], at_z((z + 3) % 4))

    def x_x(zz, hf, own=False):
        return remote(x_src(zz, hf, own), xb_at(zz, m, hf), xx_send.at[zz, hf], xx_recv.at[zz, hf], xpeer)

    def x_c(zz, hf, which, own=False):
        mm = m if which == 0 else xpeer_m
        return remote(x_src(zz, hf, own), xb_at(zz, mm, hf), xc_send.at[which, zz, hf], xc_recv.at[which, zz, hf],
                      cpeer) if which == 0 else remote(
            xb_at(zz, mm, hf), xb_at(zz, mm, hf), xc_send.at[which, zz, hf], xc_recv.at[which, zz, hf], cpeer)

    def w_cross(i, n):
        j = (xpeer_m, xdiag_m)[n]
        dev = {"mp": j, "seq": s}
        send(z == m, remote(w_src(j, i), wb_at(z, y, i), w_send.at[2 + n, i], wz_recv.at[z, i], dev))
        send(z != m, remote(w_src(j, i), tb_at(c, i), w_send.at[2 + n, i], t_recv.at[c, i], dev))

    def w_direct(i, n):
        if n == 0:
            send(m != z, remote(w_src(m, i), wb_at(z, y, i), w_send.at[0, i], wz_recv.at[z, i], at_z(m)))
        else:
            send(None, remote(w_src(cpeer_m, i), wb_at(z, y, i), w_send.at[1, i], wz_recv.at[z, i],
                              {"mp": cpeer_m, "seq": 2 * m + y}))

    def w_relay(i, n):
        cc = c if n == 0 else 1 - c
        k = (1 - x) * 2 + cc
        cp = remote(tb_at(cc, i), wb_at(z, y, i), rl_send.at[n, i], wz_recv.at[z, i], at_z(k))
        pl.when(k != z)(remote(tb_at(cc, i), tb_at(cc, i), rl_send.at[n, i], t_recv.at[cc, i], ypeer).wait_recv)
        send(k != z, cp)

    def w_along_y(n, i):
        zs = near[n]
        landed = remote(wb_at(zs, y, i), wb_at(zs, y, i), wy_send.at[n, i], wz_recv.at[zs, i], ypeer)
        if n == 0:
            pl.when(m == z)(own_w[i][1].wait)
            pl.when(m != z)(landed.wait_recv)
        else:
            landed.wait_recv()
        send(None, remote(wb_at(zs, y, i), wb_at(zs, y, i), wy_send.at[n, i], wy_recv.at[zs, i], ypeer))

    def x_step(d, hf):
        left, right = z - d, z + d
        lz, rz = (z + 4 - d) % 4, (z + d) % 4
        when(left >= 0, x_right(lz, hf).wait_recv)
        send((left >= 0) & (z < 3), x_right(lz, hf))
        send(left >= 0, x_x(lz, hf))
        send(left >= 0, x_c(lz, hf, 0))
        when(right <= 3, x_right(rz, hf).wait_recv)
        send((right <= 3) & (z > 0), x_left(rz, hf))
        send(right <= 3, x_x(rz, hf))
        send(right <= 3, x_c(rz, hf, 0))

    def x_cross(n, hf):
        zz = near[n]
        x_x(zz, hf).wait_recv()
        send(None, x_c(zz, hf, 1))

    def own_z(hf):
        send(z < 3, x_right(z, hf, True))
        send(z > 0, x_left(z, hf, True))

    def own_across(hf):
        send(None, x_x(z, hf, True))

    def own_core(hf):
        send(None, x_c(z, hf, 0, True))

    def o_half(h):
        send(None, remote(wo.at[pl.ds(h * 256, 256), :], ob.at[2 * y + h], oy_send.at[h], oy_recv.at[h], ypeer))

    def cache(n):
        for j in range(4):
            for i, (a, b) in enumerate(c_parts(j)):
                send((m == z) & (m != j), remote(a, b, c_send.at[j, i], c_recv.at[i], {"mp": j, "seq": s}))

    def norm_block(n):
        b = near[n]
        for hf in range(2):
            for which, mm in enumerate((cpeer_m, xdiag_m)):
                remote(xb_at(b, mm, hf), xb_at(b, mm, hf), xc_send.at[which, b, hf], xc_recv.at[which, b, hf],
                       cpeer).wait_recv()
        if n == 0:
            own_x.wait()

        def piece(q, carry):
            r = pl.ds(pl.multiple_of(q * 64, 64), 64)
            total = jnp.zeros((64, 1), f32)
            for mm in range(NM):
                v = xb[b, mm, r, :].astype(f32)
                total += jnp.sum(v * v, axis=-1, keepdims=True)
            scale = lax.rsqrt(total / MODEL_WIDTH + epsilon)
            for mm in range(NM):
                xn[b, mm, r, :] = (xb[b, mm, r, :].astype(f32) * scale * gain_in[mm]).astype(bf16)
            return carry

        lax.fori_loop(0, 4, piece, 0)

    def w_done(n):
        for i in range(3):
            zs = near[n]
            landed = wb_at(zs, 1 - y, i)
            remote(landed, landed, wy_send.at[n, i], wy_recv.at[zs, i], ypeer).wait_recv()

    steps = {
        "xz": own_z, "xx": own_across, "xc": own_core, "wc": w_cross, "wd": w_direct, "wo": o_half, "wr": w_relay,
        "wy": w_along_y, "xs": x_step, "xk": x_cross, "ca": cache, "nm": norm_block, "we": w_done,
    }
    for name, *rest in SCHEDULE:
        steps[name](*rest)

    def near_of(i):
        return jnp.where(i == 0, near[0], jnp.where(i == 1, near[1], jnp.where(i == 2, near[2], near[3])))

    def kv_copy(b):
        r = pl.ds(pl.multiple_of(1024 + (2 * b + y) * 256, 256), 256)
        return remote(kv.at[r, :], kv.at[r, :], kv_send.at[b], kv_recv.at[b], ypeer)

    def head_norm(g, gain, cosine, sine):
        g = g * lax.rsqrt(jnp.mean(g * g, axis=-1, keepdims=True) + epsilon) * gain
        return g * cosine + pltpu.roll(g, 64, 1) * sine

    def project(i, carry):
        b = near_of(i)
        acc = jnp.dot(xn[b, 0], wb[0], preferred_element_type=f32)
        for mm in range(1, NM):
            acc += jnp.dot(xn[b, mm], wb[mm], preferred_element_type=f32)
        r = pl.ds(pl.multiple_of(b * rows, rows), rows)
        cosine, sine = cos_t[r, :], sin_t[r, :]
        for h in range(2):
            q = head_norm(acc[:, h * 128:(h + 1) * 128], gain_q[...], cosine, sine) * query_scale
            qb[h, r, :] = q.astype(bf16)
        rk = pl.ds(pl.multiple_of(1024 + (2 * b + y) * 256, 256), 256)
        kv[rk, 0:128] = head_norm(acc[:, 256:384], gain_k[...], cosine, sine).astype(bf16)
        kv[rk, 128:256] = acc[:, 384:512].astype(bf16)
        kv_copy(b).start()
        return carry

    lax.fori_loop(0, NZ, project, 0)
    for i, (a, b) in enumerate(c_parts(0)):
        pl.when(m == z)(pltpu.make_async_copy(a, b, local_sem.at[4 + i]).wait)
        pl.when(m != z)(remote(b, b, c_send.at[0, i], c_recv.at[i], ypeer).wait_recv)

    def kv_wait(b, carry):
        r = pl.ds(pl.multiple_of(1024 + (2 * b + (1 - y)) * 256, 256), 256)
        remote(kv.at[r, :], kv.at[r, :], kv_send.at[b], kv_recv.at[b], ypeer).wait_recv()
        kv_copy(b).wait_send()
        return carry

    lax.fori_loop(0, NZ, kv_wait, 0)

    def a_copy(b, d):
        r = pl.ds(pl.multiple_of(b * rows, rows), rows)
        return remote(ab.at[m, r, :], ab.at[m, r, :], a_send.at[b, d], a_recv.at[b, m],
                      {"mp": (m + d) % 4, "seq": s})

    span = WINDOW_LENGTH + 256
    qi = lax.broadcasted_iota(jnp.int32, (rows, span), 0)
    ei = lax.broadcasted_iota(jnp.int32, (rows, span), 1)
    visible = (ei > qi) & (ei <= qi + WINDOW_LENGTH)

    def attend(b):
        r = pl.ds(pl.multiple_of(b * rows, rows), rows)
        rk = pl.ds(pl.multiple_of((2 * b + y) * 256, 256), span)
        keys = kv[rk, 0:128]
        vals = kv[rk, 128:256]
        for h in range(2):
            sc = lax.dot_general(qb[h, r, :], keys, (((1,), (1,)), ((), ())), preferred_element_type=f32)
            sc = jnp.where(visible, sc, -jnp.inf)
            top = jnp.max(sc, axis=-1, keepdims=True)
            p = jnp.exp(sc - top)
            tot = jnp.sum(p, axis=-1, keepdims=True)
            o = jnp.dot(p.astype(bf16), vals, preferred_element_type=f32)
            ab[m, r, h * 128:(h + 1) * 128] = (o / tot).astype(bf16)
        for d in range(1, 4):
            a_copy(b, d).start()

    def a_wait(b):
        r = pl.ds(pl.multiple_of(b * rows, rows), rows)
        for d in range(1, 4):
            mm = (m + d) % 4
            remote(ab.at[mm, r, :], ab.at[mm, r, :], a_send.at[b, d], a_recv.at[b, mm], ypeer).wait_recv()
            a_copy(b, d).wait_send()

    def partial(b, first, count):
        r = pl.ds(pl.multiple_of(b * rows + first, count), count)
        acc = jnp.dot(ab[0, r, :], ob[0], preferred_element_type=f32)
        for mm in range(1, NM):
            acc += jnp.dot(ab[mm, r, :], ob[mm], preferred_element_type=f32)
        return acc

    def r_copy(side, b, hf, zd):
        r = pl.ds(hf * half, half)
        return remote(sb.at[b, r, :], rb.at[side, b, r, :], r_send.at[b, hf], r_recv.at[side, b, hf], at_z(zd))

    def hop(b):
        right = b > z
        side = jnp.where(right, 0, 1)
        target = jnp.where(right, (z + 1) % 4, (z + 3) % 4)
        inner = (right & (z > 0)) | (jnp.logical_not(right) & (z < 3))
        for hf in range(2):
            r = pl.ds(hf * half, half)
            pacc[r, :] = partial(b, hf * half, half)

            @pl.when(inner)
            def _():
                r_copy(side, b, hf, target).wait_recv()
                sb[b, r, :] = (pacc[r, :] + rb[side, b, r, :].astype(f32)).astype(bf16)

            @pl.when(jnp.logical_not(inner))
            def _():
                sb[b, r, :] = pacc[r, :].astype(bf16)

            r_copy(side, b, hf, target).start()

    order = [pick(3, 3, 0, 0), pick(2, 0, 3, 1), pick(1, 2, 1, 2), z]
    edge = (z == 0) | (z == 3)

    def first_hop():
        a_wait(order[0])
        hop(order[0])

    attend(order[0])
    for h in range(2):
        o_in = ob.at[2 * (1 - y) + h]
        remote(o_in, o_in, oy_send.at[h], oy_recv.at[h], ypeer).wait_recv()
        own_o[h][1].wait()
    pl.when(edge)(first_hop)
    attend(order[1])
    pl.when(jnp.logical_not(edge))(first_hop)
    attend(order[2])
    a_wait(order[1])
    hop(order[1])
    attend(order[3])
    a_wait(order[2])
    hop(order[2])
    a_wait(order[3])

    pacc[...] = partial(z, 0, rows)
    for hf in range(2):
        r = pl.ds(hf * half, half)

        @pl.when(z > 0)
        def _():
            r_copy(0, z, hf, z).wait_recv()
            pacc[r, :] += rb[0, z, r, :].astype(f32)

        @pl.when(z < 3)
        def _():
            r_copy(1, z, hf, z).wait_recv()
            pacc[r, :] += rb[1, z, r, :].astype(f32)

    mixed = pacc[...]
    squares = jnp.broadcast_to(jnp.sum(mixed * mixed, axis=-1, keepdims=True), (rows, 128))
    ss[m] = jnp.transpose(squares)[0:8, :]

    def s_copy(d):
        return remote(ss.at[m], ss.at[m], s_send.at[d], s_recv.at[m], {"mp": (m + d) % 4, "seq": s})

    for d in range(1, 4):
        s_copy(d).start()
    for d in range(1, 4):
        mm = (m + d) % 4
        remote(ss.at[mm], ss.at[mm], s_send.at[d], s_recv.at[mm], ypeer).wait_recv()
    squares = jnp.concatenate([ss[0] + ss[1] + ss[2] + ss[3]] * 16, axis=0)
    squares = jnp.transpose(squares)[:, 0:1]
    scaling = lax.rsqrt(squares / MODEL_WIDTH + epsilon)
    out[...] = (xb[z, m].astype(f32) + mixed * scaling * gain_post[...]).astype(bf16)

    for d in range(1, 4):
        s_copy(d).wait_send()
    for d in range(4):
        for hf in range(2):
            when(z != d, r_copy(0, d, hf, (z + 1) % 4).wait_send)
    for cond, cp in pending:
        when(cond, cp.wait_send)


def fused(
    hidden_in, gain_in, w_query, key_weight, value_weight, gain_query, gain_key, start_pos,
    cached_key_rows, cached_value_rows, w_out, gain_post,
):
    rows, cols = hidden_in.shape
    depth = w_query.shape[0]
    y = lax.axis_index("seq") % 2
    block = jnp.arange(4, dtype=jnp.int32)[:, None] * 2 + y
    positions = (start_pos[0] + block * rows + jnp.arange(rows, dtype=jnp.int32)[None, :]).reshape(-1)
    inverse_freq = rope_base ** (-(jnp.arange(64, dtype=f32) * 2.0) / 128)
    angles = positions.astype(f32)[:, None] * inverse_freq[None, :]
    cosine, sine = jnp.cos(angles), jnp.sin(angles)
    cos_t = jnp.concatenate([cosine, cosine], axis=1)
    sin_t = jnp.concatenate([-sine, sine], axis=1)
    hbm = pl.BlockSpec(memory_space=pl.ANY)
    vmem = pl.BlockSpec(memory_space=pltpu.VMEM)
    dma = pltpu.SemaphoreType.DMA
    return pl.pallas_call(
        layer_kernel,
        name="layer",
        out_shape=jax.ShapeDtypeStruct((rows, cols), bf16),
        in_specs=[hbm, vmem, hbm, hbm, hbm, vmem, vmem, vmem, vmem, hbm, hbm, hbm, vmem],
        out_specs=vmem,
        scratch_shapes=[
            pltpu.VMEM((4, 4, rows, cols), bf16),
            pltpu.VMEM((4, 4, rows, cols), bf16),
            pltpu.VMEM((2, depth, 512), bf16),
            pltpu.VMEM((4, 2 * depth, 512), bf16),
            pltpu.VMEM((4, 256, cols), bf16),
            pltpu.VMEM((3072, 256), bf16),
            pltpu.VMEM((2, 1024, 128), bf16),
            pltpu.VMEM((4, 1024, 256), bf16),
            pltpu.VMEM((2, 4, rows, cols), bf16),
            pltpu.VMEM((4, rows, cols), bf16),
            pltpu.VMEM((4, 8, rows), f32),
            pltpu.VMEM((rows, cols), f32),
            dma((8,)), dma((2, 4, 2)), dma((4, 2)), dma((4, 2)), dma((4, 2)), dma((2, 4, 2)), dma((2, 4, 2)),
            dma((4, 3)), dma((2, 3)), dma((2, 3)), dma((4, 3)), dma((4, 3)), dma((4, 3)), dma((4, 2)), dma((2,)), dma((2,)), dma((2,)),
            dma((4,)), dma((4,)), dma((4, 4)), dma((4, 4)), dma((4, 2)), dma((2, 4, 2)), dma((4,)), dma((4,)),
        ],
        compiler_params=pltpu.CompilerParams(
            collective_id=0, has_side_effects=True, vmem_limit_bytes=60 * 1024 * 1024,
        ),
    )(
        hidden_in, gain_in.reshape(4, 1, cols), w_query, key_weight, value_weight,
        gain_query.reshape(1, 128), gain_key.reshape(1, 128), cos_t, sin_t,
        cached_key_rows, cached_value_rows, w_out, gain_post.reshape(1, cols),
    )


def shifted(x, axis, by):
    peers = lax.axis_size(axis)
    pairs = [(i, i + by) for i in range(peers) if 0 <= i + by < peers]
    return lax.ppermute(x, axis, pairs)


def norm_rows(values, gain):
    return values * lax.rsqrt(jnp.mean(values * values, axis=-1, keepdims=True) + epsilon) * gain


def rotate(tensor, positions):
    half_dim = tensor.shape[-1] // 2
    inverse_freq = rope_base ** (
        -(jnp.arange(half_dim, dtype=jnp.float32) * 2.0) / tensor.shape[-1]
    )
    angles = positions.astype(jnp.float32)[:, None, None] * inverse_freq[None, None, :]
    cosine = jnp.cos(angles)
    sine = jnp.sin(angles)
    first = tensor[..., :half_dim]
    second = tensor[..., half_dim:]
    return jnp.concatenate(
        [first * cosine - second * sine, second * cosine + first * sine], axis=-1
    )


def on_device(
    hidden_in,
    gain_in,
    w_query,
    key_weight,
    value_weight,
    gain_query,
    gain_key,
    start_pos,
    cached_key_rows,
    cached_value_rows,
    w_out,
    gain_post,
):
    n_rows = hidden_in.shape[0]
    head_dim = gain_query.shape[0]
    kv_cols = key_weight.shape[1]
    kv_heads = kv_cols // head_dim
    q_heads = w_query.shape[1] // head_dim
    query_group_count = q_heads // kv_heads
    full_rows = lax.all_gather(hidden_in, "mp", axis=1, tiled=True)
    normed_hidden = norm_rows(full_rows.astype(jnp.float32), gain_in).astype(jnp.bfloat16)

    def add_rows(block_rows):
        return jnp.dot(normed_hidden, block_rows, preferred_element_type=jnp.float32)

    keys_raw = add_rows(lax.all_gather(key_weight, "seq", axis=0, tiled=True))
    values_raw = add_rows(lax.all_gather(value_weight, "seq", axis=0, tiled=True))
    query_matrix = add_rows(lax.all_gather(w_query, "seq", axis=0, tiled=True))
    seq_index = lax.axis_index("seq")
    positions = start_pos[0] + seq_index * n_rows + jnp.arange(n_rows, dtype=jnp.int32)
    query_matrix = (
        rotate(norm_rows(query_matrix.reshape(n_rows, q_heads, head_dim), gain_query), positions)
        * query_scale
    ).astype(jnp.bfloat16)
    fresh_key = rotate(
        norm_rows(keys_raw.reshape(n_rows, kv_heads, head_dim), gain_key), positions
    ).astype(jnp.bfloat16)
    fresh = jnp.stack([fresh_key.reshape(n_rows, kv_cols), values_raw.astype(jnp.bfloat16)])
    reach_shards = (WINDOW_LENGTH + n_rows - 1) // n_rows
    reach_rows = reach_shards * n_rows
    pieces = []
    moving = fresh
    for hop_index in range(reach_shards):
        moving = shifted(moving, "seq", 1)
        pieces.insert(0, moving)
    prior = jnp.concatenate(pieces, axis=1)
    front_pad = reach_rows - WINDOW_LENGTH
    cached = jnp.stack([cached_key_rows, cached_value_rows])
    padded = jnp.concatenate(
        [
            jnp.zeros((2, front_pad, kv_cols), cached.dtype),
            cached,
            jnp.zeros((2, reach_rows, kv_cols), cached.dtype),
        ],
        axis=1,
    )
    cache_start = jnp.minimum(seq_index * n_rows, front_pad + WINDOW_LENGTH)
    from_cache = lax.dynamic_slice_in_dim(padded, cache_start, reach_rows, 1)
    prior_rows = jnp.arange(reach_rows, dtype=jnp.int32)
    use_cache = prior_rows < reach_rows - seq_index * n_rows
    prior = jnp.where(use_cache[None, :, None], from_cache, prior)
    window_kv = jnp.concatenate([prior, fresh], axis=1)
    span_rows = reach_rows + n_rows
    key_heads = window_kv[0].reshape(span_rows, kv_heads, head_dim)
    value_heads = window_kv[1].reshape(span_rows, kv_heads, head_dim)
    query_heads = query_matrix.reshape(n_rows, kv_heads, query_group_count, head_dim)
    scores = jnp.einsum(
        "tkgd,skd->kgts", query_heads, key_heads, preferred_element_type=jnp.float32
    )
    query_index = jnp.arange(n_rows, dtype=jnp.int32)[:, None]
    key_index = jnp.arange(span_rows, dtype=jnp.int32)[None, :]
    visible = (key_index > query_index + reach_rows - WINDOW_LENGTH) & (
        key_index <= query_index + reach_rows
    )
    scores = jnp.where(visible, scores, -jnp.inf)
    row_max = jnp.max(scores, axis=-1, keepdims=True)
    probs = jnp.exp(scores - row_max)
    totals = jnp.sum(probs, axis=-1)
    probs_b = probs.astype(jnp.bfloat16)
    summed = jnp.einsum("kgts,skd->tkgd", probs_b, value_heads, preferred_element_type=jnp.float32)
    summed = summed / jnp.transpose(totals, (2, 0, 1))[..., None]
    attn = summed.reshape(n_rows, q_heads * head_dim).astype(jnp.bfloat16)
    all_heads = lax.all_gather(attn, "mp", axis=1, tiled=True)
    projected = jnp.dot(
        all_heads,
        lax.all_gather(w_out, "seq", axis=0, tiled=True),
        preferred_element_type=jnp.float32,
    )
    squares = lax.psum(jnp.sum(projected * projected, axis=-1), "mp")
    scaling = lax.rsqrt(squares / MODEL_WIDTH + epsilon)
    return (hidden_in.astype(jnp.float32) + projected * scaling[:, None] * gain_post).astype(
        jnp.bfloat16
    )


def solution(mesh):
    in_specs = (
        P("seq", "mp"),
        P(),
        P("seq", "mp"),
        P("seq", "mp"),
        P("seq", "mp"),
        P(),
        P(),
        P(),
        P(None, "mp"),
        P(None, "mp"),
        P("seq", "mp"),
        P("mp"),
    )
    out_specs = P("seq", "mp")
    fits = mesh.shape["mp"] == 4 and mesh.shape["seq"] == 8
    return jax.shard_map(
        fused if fits else on_device, mesh=mesh, in_specs=in_specs, out_specs=out_specs, check_vma=False
    )
```

```python
import functools

import jax
import jax.numpy as jnp
import numpy as np
from jax import lax
from jax.experimental import pallas as pl
from jax.experimental.pallas import tpu as pltpu
from jax.sharding import PartitionSpec as P

MODEL_WIDTH = 5376
WINDOW_LENGTH = 1024


epsilon = 1e-06
query_scale = 168.0 ** (-0.5)
rope_base = 10000.0

MESH = pl.DeviceIdType.MESH
f32 = jnp.float32
bf16 = jnp.bfloat16


SCHEDULE = (
    ("xz", 0), ("wc", 0, 0), ("wo", 1), ("wc", 0, 1), ("xz", 1), ("gp", 0), ("tr", 0), ("xr", 1, 0),
    ("wc", 2, 0), ("xl", 1, 0), ("wo", 0), ("wd", 0, 0), ("xx", 0), ("wc", 1, 0), ("wy", 0, 0), ("wc", 1, 1),
    ("wc", 2, 1), ("wr", 0, 1), ("xl", 1, 1), ("xx", 1), ("xr", 1, 1), ("wd", 0, 1), ("tr", 1), ("tr", 2),
    ("tr", 3), ("wr", 0, 0), ("xl", 2, 0), ("xr", 2, 0), ("wy", 0, 2), ("wy", 0, 1), ("wy", 3, 0), ("xc", 0),
    ("wd", 2, 0), ("wr", 2, 1), ("wy", 1, 0), ("wd", 2, 1), ("wr", 2, 0), ("wd", 1, 1), ("od", 1), ("wr", 1, 1),
    ("wy", 2, 0), ("xk", 1, 1), ("xl", 2, 1), ("xr", 2, 1), ("xr", 3, 0), ("xk", 0, 0), ("wy", 1, 2),
    ("xk", 2, 0), ("we", 3, 0), ("wy", 3, 2), ("xk", 1, 0), ("xl", 3, 0), ("wy", 2, 2), ("xk", 2, 1), ("nm", 1),
    ("xk", 3, 0), ("xr", 3, 1), ("wr", 1, 0), ("xl", 3, 1), ("wd", 1, 0), ("wy", 1, 1), ("xc", 1), ("we", 0, 0),
    ("xk", 0, 1), ("we", 0, 1), ("wy", 3, 1), ("wy", 2, 1), ("od", 0), ("xk", 3, 1), ("nm", 2), ("we", 2, 0),
    ("we", 1, 0), ("nm", 0), ("we", 1, 1), ("wm", 0), ("ca", 0), ("we", 3, 1), ("we", 2, 1), ("wm", 1),
    ("pk", 1), ("pk", 2), ("pq", 0), ("nm", 3), ("kd", 1), ("pk", 3), ("pk", 0), ("pq", 3), ("cd", 0),
    ("kd", 3), ("kd", 2), ("kd", 0), ("at", 0, 1), ("at", 0, 0), ("pq", 1), ("pq", 2), ("he", 0), ("at", 1, 0),
    ("at", 1, 1), ("at", 2, 0), ("hi", 0), ("at", 2, 1), ("hp", 1), ("hp", 2), ("at", 3, 1), ("at", 3, 0),
)


def layer_kernel(
    hidden, gain_in, wq, wk, wv, gain_q, gain_k, start, freq, cache_k, cache_v, wo, gain_post,
    out,
    cos_t, sin_t, g_in, g_post, xb, xn, tb, wb, wrem, ob, kv, qb, ab, rb, sb, ss, pacc,
    local_sem, xz_send, xz_recv, xx_send, xx_recv, xc_send, xc_recv,
    w_send, t_recv, rl_send, wz_recv, wy_send, wy_recv, c_send, c_recv, oy_send, oy_recv,
    kv_send, kv_recv, a_send, a_recv, r_send, r_recv, s_send, s_recv,
):
    NZ, NM = 4, 4
    cols, rows = hidden.shape
    depth = wq.shape[0]
    m = lax.axis_index("mp")
    s = lax.axis_index("seq")
    z, y = s // 2, s % 2
    x, c = m // 2, m % 2
    ypeer = {"mp": m, "seq": 2 * z + (1 - y)}
    xpeer_m = (1 - x) * 2 + c
    cpeer_m = x * 2 + (1 - c)
    xdiag_m = (1 - x) * 2 + (1 - c)
    xpeer = {"mp": xpeer_m, "seq": s}
    cpeer = {"mp": cpeer_m, "seq": s}

    def at_z(zz):
        return {"mp": m, "seq": 2 * zz + y}

    def remote(src, dst, send, recv, dev):
        return pltpu.make_async_remote_copy(
            src_ref=src, dst_ref=dst, send_sem=send, recv_sem=recv,
            device_id=dev, device_id_type=MESH)

    def pick(a0, a1, a2, a3):
        return jnp.where(z == 0, a0, jnp.where(z == 1, a1, jnp.where(z == 2, a2, a3)))

    near = [z, pick(1, 0, 1, 2), pick(2, 2, 3, 1), pick(3, 3, 0, 0)]

    barrier = pltpu.get_barrier_semaphore()
    for d in range(1, 4):
        pl.semaphore_signal(barrier, inc=1, device_id=at_z((z + d) % 4), device_id_type=MESH)
        pl.semaphore_signal(
            barrier, inc=1, device_id={"mp": cpeer_m, "seq": 2 * ((z + d) % 4) + y}, device_id_type=MESH)
        pl.semaphore_signal(barrier, inc=1, device_id={"mp": (m + d) % 4, "seq": s}, device_id_type=MESH)
    pl.semaphore_signal(barrier, inc=1, device_id=ypeer, device_id_type=MESH)

    spans = [(0, 256), (256, 128), (384, 128)]

    def w_src(j, i):
        width = spans[i][1]
        return (wq, wk, wv)[i].at[:, pl.ds(pl.multiple_of(j * width, 128), width)]

    def wb_at(zsrc, yy, i):
        return wb.at[zsrc, pl.ds(pl.multiple_of(yy * depth, 16), depth), pl.ds(*spans[i])]

    def tb_at(k, i):
        return tb.at[k, :, pl.ds(*spans[i])]

    def c_parts(j):
        return [
            (cache_k.at[:, pl.ds(j * 128, 128)], kv.at[pl.ds(0, 1024), pl.ds(0, 128)]),
            (cache_v.at[:, pl.ds(j * 128, 128)], kv.at[pl.ds(0, 1024), pl.ds(128, 128)]),
        ]

    half = rows // 2
    full = cols // 128
    main = full * 128

    def h_src(hf):
        return hidden.at[:, pl.ds(hf * half, half)]

    own_x = [(None, pltpu.make_async_copy(h_src(hf), xb.at[z, m, hf], local_sem.at[8 + hf])) for hf in range(2)]
    own_w = [
        (m == z, pltpu.make_async_copy(w_src(m, i), wb_at(z, y, i), local_sem.at[1 + i])) for i in range(3)
    ]
    own_c = []
    for j in range(4):
        mine = (m == j) & (z == j)
        own_c.extend((mine, pltpu.make_async_copy(a, b, local_sem.at[4 + i])) for i, (a, b) in enumerate(c_parts(j)))
    own_o = [
        (None, pltpu.make_async_copy(wo.at[:, pl.ds(h * 256, 256)], ob.at[2 * y + h], local_sem.at[6 + h]))
        for h in range(2)
    ]

    def when(cond, fn):
        if cond is None:
            fn()
        else:
            pl.when(cond)(fn)

    for cond, cp in own_x + own_w + own_c + own_o:
        when(cond, cp.start)

    pl.semaphore_wait(barrier, 10)

    pending = []

    def send(cond, cp):
        when(cond, cp.start)
        pending.append((cond, cp))

    def xb_at(zz, mm, hf):
        return xb.at[zz, mm, hf]

    def x_src(zz, hf, own):
        return h_src(hf) if own else xb_at(zz, m, hf)

    def x_right(zz, hf, own=False):
        return remote(
            x_src(zz, hf, own), xb_at(zz, m, hf), xz_send.at[0, zz, hf], xz_recv.at[zz, hf], at_z((z + 1) % 4))

    def x_left(zz, hf, own=False):
        return remote(
            x_src(zz, hf, own), xb_at(zz, m, hf), xz_send.at[1, zz, hf], xz_recv.at[zz, hf], at_z((z + 3) % 4))

    def x_x(zz, hf, own=False):
        return remote(x_src(zz, hf, own), xb_at(zz, m, hf), xx_send.at[zz, hf], xx_recv.at[zz, hf], xpeer)

    def x_c(zz, hf, which, own=False):
        mm = m if which == 0 else xpeer_m
        return remote(h_src(hf) if own else xb_at(zz, mm, hf), xb_at(zz, mm, hf), xc_send.at[which, zz, hf],
                      xc_recv.at[which, zz, hf], cpeer)

    def w_cross(i, n):
        j = (xpeer_m, xdiag_m)[n]
        dev = {"mp": j, "seq": s}
        send(z == m, remote(w_src(j, i), wb_at(z, y, i), w_send.at[2 + n, i], wz_recv.at[z, i], dev))
        send(z != m, remote(w_src(j, i), tb_at(c, i), w_send.at[2 + n, i], t_recv.at[c, i], dev))

    def w_direct(i, n):
        if n == 0:
            send(m != z, remote(w_src(m, i), wb_at(z, y, i), w_send.at[0, i], wz_recv.at[z, i], at_z(m)))
        else:
            send(None, remote(w_src(cpeer_m, i), wb_at(z, y, i), w_send.at[1, i], wz_recv.at[z, i],
                              {"mp": cpeer_m, "seq": 2 * m + y}))

    def w_relay(i, n):
        cc = c if n == 0 else 1 - c
        k = (1 - x) * 2 + cc
        cp = remote(tb_at(cc, i), wb_at(z, y, i), rl_send.at[n, i], wz_recv.at[z, i], at_z(k))
        pl.when(k != z)(remote(tb_at(cc, i), tb_at(cc, i), rl_send.at[n, i], t_recv.at[cc, i], ypeer).wait_recv)
        send(k != z, cp)

    def w_along_y(n, i):
        zs = near[n]
        landed = remote(wb_at(zs, y, i), wb_at(zs, y, i), wy_send.at[n, i], wz_recv.at[zs, i], ypeer)
        if n == 0:
            pl.when(m == z)(own_w[i][1].wait)
            pl.when(m != z)(landed.wait_recv)
        else:
            landed.wait_recv()
        send(None, remote(wb_at(zs, y, i), wb_at(zs, y, i), wy_send.at[n, i], wy_recv.at[zs, i], ypeer))

    def from_left(d, hf):
        left = z - d
        lz = (z + 4 - d) % 4
        when(left >= 0, x_right(lz, hf).wait_recv)
        send((left >= 0) & (z < 3), x_right(lz, hf))
        send(left >= 0, x_x(lz, hf))
        send(left >= 0, x_c(lz, hf, 0))

    def from_right(d, hf):
        right = z + d
        rz = (z + d) % 4
        when(right <= 3, x_right(rz, hf).wait_recv)
        send((right <= 3) & (z > 0), x_left(rz, hf))
        send(right <= 3, x_x(rz, hf))
        send(right <= 3, x_c(rz, hf, 0))

    def x_cross(n, hf):
        zz = near[n]
        x_x(zz, hf).wait_recv()
        send(None, x_c(zz, hf, 1))

    def own_z(hf):
        send(z < 3, x_right(z, hf, True))
        send(z > 0, x_left(z, hf, True))

    def own_across(hf):
        send(None, x_x(z, hf, True))

    def own_core(hf):
        send(None, x_c(z, hf, 0, True))

    def o_half(h):
        send(None, remote(wo.at[:, pl.ds(h * 256, 256)], ob.at[2 * y + h], oy_send.at[h], oy_recv.at[h], ypeer))

    def cache(n):
        for j in range(4):
            for i, (a, b) in enumerate(c_parts(j)):
                send((m == z) & (m != j), remote(a, b, c_send.at[j, i], c_recv.at[i], {"mp": j, "seq": s}))

    def norm_block(n):
        b = near[n]
        for hf in range(2):
            for which, mm in enumerate((cpeer_m, xdiag_m)):
                remote(xb_at(b, mm, hf), xb_at(b, mm, hf), xc_send.at[which, b, hf], xc_recv.at[which, b, hf],
                       cpeer).wait_recv()
        if n == 0:
            for _, cp in own_x:
                cp.wait()

        def piece(hf, carry):
            def squares(mm, total):
                v = xb[b, mm, hf].astype(f32)
                return total + jnp.sum((v * v).reshape(cols // 32, 32, 128), axis=0)

            total = lax.fori_loop(0, NM, squares, jnp.zeros((32, 128), f32))
            scale = lax.rsqrt(jnp.sum(total, axis=0, keepdims=True) / MODEL_WIDTH + epsilon)
            scale = jnp.transpose(jnp.broadcast_to(scale, (half, 128)))
            r = pl.ds(pl.multiple_of(hf * half, half), half)
            for t in range(NM * full + 2):
                if t < NM * full:
                    v = xb[b, t // full, hf, t % full * 128:(t % full + 1) * 128, :]
                else:
                    i = 2 * (t - NM * full)
                    v = jnp.concatenate([xb[b, i, hf, main:cols, :], xb[b, i + 1, hf, main:cols, :]], axis=0)
                v = jnp.transpose(v).astype(f32)
                xn[b, r, t * 128:(t + 1) * 128] = (v * scale * g_in[t:t + 1, :]).astype(bf16)
            return carry

        lax.fori_loop(0, 2, piece, 0)

    def angles(n):
        b = near[n]
        r = pl.ds(pl.multiple_of(b * rows, rows), rows)
        place = start[0] + (2 * b + y) * rows + lax.broadcasted_iota(jnp.int32, (rows, 128), 0)
        angle = place.astype(f32) * freq[...]
        lane = lax.broadcasted_iota(jnp.int32, (rows, 128), 1)
        sine = jnp.sin(angle)
        cos_t[r, :] = jnp.cos(angle)
        sin_t[r, :] = jnp.where(lane < 64, -sine, sine)

    def gains(n):
        lane = lax.broadcasted_iota(jnp.int32, (1, 128), 1)
        for mm in range(NM):
            base = mm * cols // 128
            for t in range(full):
                g = gain_in[base + t:base + t + 1, :]
                if mm % 2:
                    g = pltpu.roll(jnp.where(lane < 64, gain_in[base + t + 1:base + t + 2, :], g), 64, 1)
                g_in[mm * full + t:mm * full + t + 1, :] = g
        for i in range(2):
            low = 2 * i * cols // 128 + full
            g_in[NM * full + i:NM * full + i + 1, :] = jnp.where(
                lane < 64, gain_in[low:low + 1, :], gain_in[low + full:low + full + 1, :])
        for t in range(full + 1):
            width = min(128, cols - t * 128)
            g = jnp.broadcast_to(gain_post[:, t * 128:t * 128 + width], (128, width))
            g_post[t * 128:t * 128 + width, :] = jnp.transpose(g)

    def w_done(n, part):
        zs = near[n]
        for i in ((0,), (1, 2))[part]:
            landed = wb_at(zs, 1 - y, i)
            remote(landed, landed, wy_send.at[n, i], wy_recv.at[zs, i], ypeer).wait_recv()

    def w_ends(part):
        for mm in range(NM):
            wrem[mm * 64:(mm + 1) * 64, part * 256:(part + 1) * 256] = wb[mm, main:cols, part * 256:(part + 1) * 256]

    def o_done(h):
        o_in = ob.at[2 * (1 - y) + h]
        remote(o_in, o_in, oy_send.at[h], oy_recv.at[h], ypeer).wait_recv()
        own_o[h][1].wait()

    def c_done(n):
        for i, (a, b) in enumerate(c_parts(0)):
            pl.when(m == z)(pltpu.make_async_copy(a, b, local_sem.at[4 + i]).wait)
            pl.when(m != z)(remote(b, b, c_send.at[0, i], c_recv.at[i], ypeer).wait_recv)

    def kv_copy(b):
        r = pl.ds(pl.multiple_of(1024 + (2 * b + y) * 256, 256), 256)
        return remote(kv.at[r, :], kv.at[r, :], kv_send.at[b], kv_recv.at[b], ypeer)

    def head_norm(g, gain, cosine, sine):
        g = g * lax.rsqrt(jnp.mean(g * g, axis=-1, keepdims=True) + epsilon) * gain
        return g * cosine + pltpu.roll(g, 64, 1) * sine

    def product(b, part):
        c = slice(part * 256, (part + 1) * 256)
        acc = jnp.dot(xn[b, :, NM * main:NM * cols], wrem[:, c], preferred_element_type=f32)
        for mm in range(NM):
            acc += jnp.dot(xn[b, :, mm * main:(mm + 1) * main], wb[mm, 0:main, c], preferred_element_type=f32)
        return acc

    def project_q(n):
        b = near[n]
        acc = product(b, 0)
        r = pl.ds(pl.multiple_of(b * rows, rows), rows)
        cosine, sine = cos_t[r, :], sin_t[r, :]
        for h in range(2):
            q = head_norm(acc[:, h * 128:(h + 1) * 128], gain_q[...], cosine, sine) * query_scale
            qb[h, r, :] = q.astype(bf16)

    def project_kv(n):
        b = near[n]
        acc = product(b, 1)
        r = pl.ds(pl.multiple_of(b * rows, rows), rows)
        rk = pl.ds(pl.multiple_of(1024 + (2 * b + y) * 256, 256), 256)
        kv[rk, 0:128] = head_norm(acc[:, 0:128], gain_k[...], cos_t[r, :], sin_t[r, :]).astype(bf16)
        kv[rk, 128:256] = acc[:, 128:256].astype(bf16)
        send(None, kv_copy(b))

    def kv_done(n):
        b = near[n]
        r = pl.ds(pl.multiple_of(1024 + (2 * b + (1 - y)) * 256, 256), 256)
        remote(kv.at[r, :], kv.at[r, :], kv_send.at[b], kv_recv.at[b], ypeer).wait_recv()

    def a_copy(b, d, h):
        r = pl.ds(pl.multiple_of(b * rows, rows), rows)
        piece = ab.at[m, r, pl.ds(h * 128, 128)]
        return remote(piece, piece, a_send.at[b, d, h], a_recv.at[b, m, h], {"mp": (m + d) % 4, "seq": s})

    span = WINDOW_LENGTH + 256
    qi = lax.broadcasted_iota(jnp.int32, (rows, span), 0)
    ei = lax.broadcasted_iota(jnp.int32, (rows, span), 1)
    visible = (ei > qi) & (ei <= qi + WINDOW_LENGTH)
    order = [pick(3, 3, 0, 0), pick(2, 0, 3, 1), pick(1, 2, 1, 2), z]
    edge = (z == 0) | (z == 3)

    def attend(k, h):
        b = order[k]
        r = pl.ds(pl.multiple_of(b * rows, rows), rows)
        rk = pl.ds(pl.multiple_of((2 * b + y) * 256, 256), span)
        keys = kv[rk, 0:128]
        vals = kv[rk, 128:256]
        sc = lax.dot_general(qb[h, r, :], keys, (((1,), (1,)), ((), ())), preferred_element_type=f32)
        sc = jnp.where(visible, sc, -jnp.inf)
        top = jnp.max(sc, axis=-1, keepdims=True)
        p = jnp.exp(sc - top)
        tot = jnp.sum(p, axis=-1, keepdims=True)
        o = jnp.dot(p.astype(bf16), vals, preferred_element_type=f32)
        ab[m, r, h * 128:(h + 1) * 128] = (o / tot).astype(bf16)
        for d in (2, 3, 1):
            send(None, a_copy(b, d, h))

    def a_wait(b):
        r = pl.ds(pl.multiple_of(b * rows, rows), rows)
        for h in range(2):
            for d in range(1, 4):
                mm = (m + d) % 4
                piece = ab.at[mm, r, pl.ds(h * 128, 128)]
                remote(piece, piece, a_send.at[b, d, h], a_recv.at[b, mm, h], ypeer).wait_recv()

    def partial(b):
        r = pl.ds(pl.multiple_of(b * rows, rows), rows)
        acc = None
        for mm in range(NM):
            term = lax.dot_general(ob[mm], ab[mm, r, :], (((1,), (1,)), ((), ())), preferred_element_type=f32)
            acc = term if acc is None else acc + term
        for hf in range(2):
            pacc[hf] = acc[:, hf * half:(hf + 1) * half]

    def r_copy(side, b, hf, zd):
        return remote(sb.at[b, hf], rb.at[side, b, hf], r_send.at[b, hf], r_recv.at[side, b, hf], at_z(zd))

    def hop(b):
        right = b > z
        side = jnp.where(right, 0, 1)
        target = jnp.where(right, (z + 1) % 4, (z + 3) % 4)
        inner = (right & (z > 0)) | (jnp.logical_not(right) & (z < 3))
        partial(b)
        for hf in range(2):
            @pl.when(inner)
            def _():
                r_copy(side, b, hf, target).wait_recv()
                sb[b, hf] = (pacc[hf] + rb[side, b, hf].astype(f32)).astype(bf16)

            @pl.when(jnp.logical_not(inner))
            def _():
                sb[b, hf] = pacc[hf].astype(bf16)

            r_copy(side, b, hf, target).start()

    def hop_step(k):
        a_wait(order[k])
        hop(order[k])

    def hop_edge(k):
        pl.when(edge)(lambda: hop_step(k))

    def hop_inner(k):
        pl.when(jnp.logical_not(edge))(lambda: hop_step(k))

    steps = {
        "xz": own_z, "xx": own_across, "xc": own_core, "wc": w_cross, "wd": w_direct, "wo": o_half, "wr": w_relay,
        "wy": w_along_y, "xl": from_left, "xr": from_right, "xk": x_cross, "ca": cache, "nm": norm_block,
        "we": w_done, "wm": w_ends, "od": o_done, "cd": c_done, "pq": project_q, "pk": project_kv, "kd": kv_done,
        "tr": angles, "gp": gains, "at": attend, "he": hop_edge, "hi": hop_inner, "hp": hop_step,
    }
    for name, *rest in SCHEDULE:
        steps[name](*rest)

    a_wait(order[3])

    partial(z)

    def add_arrived(side, hf):
        r_copy(side, z, hf, z).wait_recv()
        pacc[hf] += rb[side, z, hf].astype(f32)

    for hf in range(2):
        pl.when(z > 0)(functools.partial(add_arrived, 0, hf))
        pl.when(z < 3)(functools.partial(add_arrived, 1, hf))
        mixed = pacc[hf]
        squares = jnp.sum(mixed * mixed, axis=0, keepdims=True)
        ss[m, :, hf * half:(hf + 1) * half] = jnp.broadcast_to(squares, (8, half))

    def s_copy(d):
        return remote(ss.at[m], ss.at[m], s_send.at[d], s_recv.at[m], {"mp": (m + d) % 4, "seq": s})

    for d in range(1, 4):
        s_copy(d).start()
    for d in range(1, 4):
        mm = (m + d) % 4
        remote(ss.at[mm], ss.at[mm], s_send.at[d], s_recv.at[mm], ypeer).wait_recv()
    squares = (ss[0] + ss[1] + ss[2] + ss[3])[0:1, :]
    scaling = lax.rsqrt(squares / MODEL_WIDTH + epsilon)
    for hf in range(2):
        part = slice(hf * half, (hf + 1) * half)
        out[:, part] = (xb[z, m, hf].astype(f32) + pacc[hf] * scaling[:, part] * g_post[...]).astype(bf16)

    for d in range(1, 4):
        s_copy(d).wait_send()
    for d in range(4):
        for hf in range(2):
            when(z != d, r_copy(0, d, hf, (z + 1) % 4).wait_send)
    for cond, cp in pending:
        when(cond, cp.wait_send)


def fused(
    hidden_in, gain_in, w_query, key_weight, value_weight, gain_query, gain_key, start_pos,
    cached_key_rows, cached_value_rows, w_out, gain_post,
):
    rows, cols = hidden_in.shape
    depth = w_query.shape[0]
    inverse_freq = rope_base ** (-(np.arange(64) * 2.0) / 128)
    freq = jnp.asarray(np.concatenate([inverse_freq, inverse_freq])[None, :], f32)
    hbm = pl.BlockSpec(memory_space=pl.ANY)
    vmem = pl.BlockSpec(memory_space=pltpu.VMEM)
    smem = pl.BlockSpec(memory_space=pltpu.SMEM)
    dma = pltpu.SemaphoreType.DMA
    turned = pl.pallas_call(
        layer_kernel,
        name="layer",
        out_shape=jax.ShapeDtypeStruct((cols, rows), bf16),
        in_specs=[hbm, vmem, hbm, hbm, hbm, vmem, vmem, smem, vmem, hbm, hbm, hbm, vmem],
        out_specs=vmem,
        scratch_shapes=[
            pltpu.VMEM((1024, 128), f32),
            pltpu.VMEM((1024, 128), f32),
            pltpu.VMEM((4 * cols // 128, 128), f32),
            pltpu.VMEM((cols, 128), f32),
            pltpu.VMEM((4, 4, 2, cols, 128), bf16),
            pltpu.VMEM((4, rows, 4 * cols), bf16),
            pltpu.VMEM((2, depth, 512), bf16),
            pltpu.VMEM((4, 2 * depth, 512), bf16),
            pltpu.VMEM((256, 512), bf16),
            pltpu.VMEM((4, cols, 256), bf16),
            pltpu.VMEM((3072, 256), bf16),
            pltpu.VMEM((2, 1024, 128), bf16),
            pltpu.VMEM((4, 1024, 256), bf16),
            pltpu.VMEM((2, 4, 2, cols, 128), bf16),
            pltpu.VMEM((4, 2, cols, 128), bf16),
            pltpu.VMEM((4, 8, rows), f32),
            pltpu.VMEM((2, cols, 128), f32),
            dma((10,)), dma((2, 4, 2)), dma((4, 2)), dma((4, 2)), dma((4, 2)), dma((2, 4, 2)), dma((2, 4, 2)),
            dma((4, 3)), dma((2, 3)), dma((2, 3)), dma((4, 3)), dma((4, 3)), dma((4, 3)), dma((4, 2)), dma((2,)), dma((2,)), dma((2,)),
            dma((4,)), dma((4,)), dma((4, 4, 2)), dma((4, 4, 2)), dma((4, 2)), dma((2, 4, 2)), dma((4,)), dma((4,)),
        ],
        compiler_params=pltpu.CompilerParams(
            collective_id=0, has_side_effects=True, vmem_limit_bytes=60 * 1024 * 1024,
        ),
    )(
        hidden_in.T, gain_in.reshape(-1, 128), w_query, key_weight, value_weight,
        gain_query.reshape(1, 128), gain_key.reshape(1, 128), start_pos, freq,
        cached_key_rows, cached_value_rows, w_out.T, gain_post.reshape(1, cols),
    )
    return turned.T


def shifted(x, axis, by):
    peers = lax.axis_size(axis)
    pairs = [(i, i + by) for i in range(peers) if 0 <= i + by < peers]
    return lax.ppermute(x, axis, pairs)


def norm_rows(values, gain):
    return values * lax.rsqrt(jnp.mean(values * values, axis=-1, keepdims=True) + epsilon) * gain


def rotate(tensor, positions):
    half_dim = tensor.shape[-1] // 2
    inverse_freq = rope_base ** (
        -(jnp.arange(half_dim, dtype=jnp.float32) * 2.0) / tensor.shape[-1]
    )
    angles = positions.astype(jnp.float32)[:, None, None] * inverse_freq[None, None, :]
    cosine = jnp.cos(angles)
    sine = jnp.sin(angles)
    first = tensor[..., :half_dim]
    second = tensor[..., half_dim:]
    return jnp.concatenate(
        [first * cosine - second * sine, second * cosine + first * sine], axis=-1
    )


def on_device(
    hidden_in,
    gain_in,
    w_query,
    key_weight,
    value_weight,
    gain_query,
    gain_key,
    start_pos,
    cached_key_rows,
    cached_value_rows,
    w_out,
    gain_post,
):
    n_rows = hidden_in.shape[0]
    head_dim = gain_query.shape[0]
    kv_cols = key_weight.shape[1]
    kv_heads = kv_cols // head_dim
    q_heads = w_query.shape[1] // head_dim
    query_group_count = q_heads // kv_heads
    full_rows = lax.all_gather(hidden_in, "mp", axis=1, tiled=True)
    normed_hidden = norm_rows(full_rows.astype(jnp.float32), gain_in).astype(jnp.bfloat16)

    def add_rows(block_rows):
        return jnp.dot(normed_hidden, block_rows, preferred_element_type=jnp.float32)

    keys_raw = add_rows(lax.all_gather(key_weight, "seq", axis=0, tiled=True))
    values_raw = add_rows(lax.all_gather(value_weight, "seq", axis=0, tiled=True))
    query_matrix = add_rows(lax.all_gather(w_query, "seq", axis=0, tiled=True))
    seq_index = lax.axis_index("seq")
    positions = start_pos[0] + seq_index * n_rows + jnp.arange(n_rows, dtype=jnp.int32)
    query_matrix = (
        rotate(norm_rows(query_matrix.reshape(n_rows, q_heads, head_dim), gain_query), positions)
        * query_scale
    ).astype(jnp.bfloat16)
    fresh_key = rotate(
        norm_rows(keys_raw.reshape(n_rows, kv_heads, head_dim), gain_key), positions
    ).astype(jnp.bfloat16)
    fresh = jnp.stack([fresh_key.reshape(n_rows, kv_cols), values_raw.astype(jnp.bfloat16)])
    reach_shards = (WINDOW_LENGTH + n_rows - 1) // n_rows
    reach_rows = reach_shards * n_rows
    pieces = []
    moving = fresh
    for hop_index in range(reach_shards):
        moving = shifted(moving, "seq", 1)
        pieces.insert(0, moving)
    prior = jnp.concatenate(pieces, axis=1)
    front_pad = reach_rows - WINDOW_LENGTH
    cached = jnp.stack([cached_key_rows, cached_value_rows])
    padded = jnp.concatenate(
        [
            jnp.zeros((2, front_pad, kv_cols), cached.dtype),
            cached,
            jnp.zeros((2, reach_rows, kv_cols), cached.dtype),
        ],
        axis=1,
    )
    cache_start = jnp.minimum(seq_index * n_rows, front_pad + WINDOW_LENGTH)
    from_cache = lax.dynamic_slice_in_dim(padded, cache_start, reach_rows, 1)
    prior_rows = jnp.arange(reach_rows, dtype=jnp.int32)
    use_cache = prior_rows < reach_rows - seq_index * n_rows
    prior = jnp.where(use_cache[None, :, None], from_cache, prior)
    window_kv = jnp.concatenate([prior, fresh], axis=1)
    span_rows = reach_rows + n_rows
    key_heads = window_kv[0].reshape(span_rows, kv_heads, head_dim)
    value_heads = window_kv[1].reshape(span_rows, kv_heads, head_dim)
    query_heads = query_matrix.reshape(n_rows, kv_heads, query_group_count, head_dim)
    scores = jnp.einsum(
        "tkgd,skd->kgts", query_heads, key_heads, preferred_element_type=jnp.float32
    )
    query_index = jnp.arange(n_rows, dtype=jnp.int32)[:, None]
    key_index = jnp.arange(span_rows, dtype=jnp.int32)[None, :]
    visible = (key_index > query_index + reach_rows - WINDOW_LENGTH) & (
        key_index <= query_index + reach_rows
    )
    scores = jnp.where(visible, scores, -jnp.inf)
    row_max = jnp.max(scores, axis=-1, keepdims=True)
    probs = jnp.exp(scores - row_max)
    totals = jnp.sum(probs, axis=-1)
    probs_b = probs.astype(jnp.bfloat16)
    summed = jnp.einsum("kgts,skd->tkgd", probs_b, value_heads, preferred_element_type=jnp.float32)
    summed = summed / jnp.transpose(totals, (2, 0, 1))[..., None]
    attn = summed.reshape(n_rows, q_heads * head_dim).astype(jnp.bfloat16)
    all_heads = lax.all_gather(attn, "mp", axis=1, tiled=True)
    projected = jnp.dot(
        all_heads,
        lax.all_gather(w_out, "seq", axis=0, tiled=True),
        preferred_element_type=jnp.float32,
    )
    squares = lax.psum(jnp.sum(projected * projected, axis=-1), "mp")
    scaling = lax.rsqrt(squares / MODEL_WIDTH + epsilon)
    return (hidden_in.astype(jnp.float32) + projected * scaling[:, None] * gain_post).astype(
        jnp.bfloat16
    )


def solution(mesh):
    in_specs = (
        P("seq", "mp"),
        P(),
        P("seq", "mp"),
        P("seq", "mp"),
        P("seq", "mp"),
        P(),
        P(),
        P(),
        P(None, "mp"),
        P(None, "mp"),
        P("seq", "mp"),
        P("mp"),
    )
    out_specs = P("seq", "mp")
    fits = mesh.shape["mp"] == 4 and mesh.shape["seq"] == 8
    return jax.shard_map(
        fused if fits else on_device, mesh=mesh, in_specs=in_specs, out_specs=out_specs, check_vma=False
    )
```

```python
import functools

import jax
import jax.numpy as jnp
import numpy as np
from jax import lax
from jax.experimental import pallas as pl
from jax.experimental.pallas import tpu as pltpu
from jax.sharding import PartitionSpec as P

MODEL_WIDTH = 5376
WINDOW_LENGTH = 1024


epsilon = 1e-06
query_scale = 168.0 ** (-0.5)
rope_base = 10000.0

MESH = pl.DeviceIdType.MESH
f32 = jnp.float32
bf16 = jnp.bfloat16


SCHEDULE = (
    ("wc", 0, 0), ("wo", 1), ("xz", 0), ("wc", 0, 1), ("wc", 2, 0), ("xz", 1), ("wc", 1, 0), ("gp", 0),
    ("xl", 1, 0), ("xr", 1, 0), ("wy", 0, 0), ("xx", 0), ("wd", 0, 0), ("tr", 0), ("wc", 2, 1), ("wc", 1, 1),
    ("wr", 0, 0), ("tr", 2), ("wr", 0, 1), ("xl", 1, 1), ("wo", 0), ("xx", 1), ("xr", 1, 1), ("wd", 0, 1),
    ("wy", 0, 1), ("xc", 0), ("wy", 0, 2), ("xl", 2, 0), ("wr", 2, 0), ("xk", 0, 0), ("tr", 3), ("xr", 2, 0),
    ("wy", 3, 0), ("wd", 2, 0), ("wr", 2, 1), ("wy", 1, 0), ("wd", 2, 1), ("wd", 1, 1), ("tr", 1), ("we", 3, 0),
    ("wy", 2, 0), ("od", 1), ("xk", 1, 1), ("wr", 1, 1), ("xr", 2, 1), ("xk", 1, 0), ("xl", 2, 1), ("wy", 1, 2),
    ("xk", 2, 0), ("od", 0), ("xr", 3, 0), ("wy", 3, 2), ("xl", 3, 0), ("xk", 2, 1), ("wy", 2, 2), ("nm", 1),
    ("xk", 0, 1), ("xk", 3, 0), ("wr", 1, 0), ("xl", 3, 1), ("xr", 3, 1), ("wd", 1, 0), ("we", 0, 0),
    ("wy", 1, 1), ("xc", 1), ("we", 0, 1), ("nm", 2), ("ca", 0), ("wy", 3, 1), ("we", 2, 0), ("wy", 2, 1),
    ("we", 1, 1), ("ca", 1), ("xk", 3, 1), ("we", 1, 0), ("wm", 0), ("nm", 0), ("we", 2, 1), ("we", 3, 1),
    ("wm", 1), ("pk", 0, 3), ("nm", 3), ("pk", 3, 4), ("cd", 0), ("pq", 3, 4), ("kd", 0), ("pq", 0, 3),
    ("kd", 1), ("kd", 2), ("kd", 3), ("cd", 1), ("at", 0, 0), ("at", 0, 1), ("he", 0), ("at", 1, 0),
    ("at", 1, 1), ("at", 2, 1), ("hi", 0), ("at", 2, 0), ("hp", 1), ("hp", 2), ("at", 3, 0), ("at", 3, 1),
)


def layer_kernel(
    hidden, gain_in, wq, wk, wv, gain_q, gain_k, start, freq, cache_k, cache_v, wo, gain_post,
    out,
    cos_t, sin_t, g_in, g_post, xb, xn, tb, wb, wrem, ob, kv, qb, ab, rb, sb, ss, pacc,
    local_sem, xz_send, xz_recv, xx_send, xx_recv, xc_send, xc_recv,
    w_send, t_recv, rl_send, wz_recv, wy_send, wy_recv, c_send, c_recv, oy_send, oy_recv,
    kv_send, kv_recv, a_send, a_recv, r_send, r_recv, s_send, s_recv,
):
    NZ, NM = 4, 4
    cols, rows = hidden.shape
    depth = wq.shape[0]
    m = lax.axis_index("mp")
    s = lax.axis_index("seq")
    z, y = s // 2, s % 2
    x, c = m // 2, m % 2
    ypeer = {"mp": m, "seq": 2 * z + (1 - y)}
    xpeer_m = (1 - x) * 2 + c
    cpeer_m = x * 2 + (1 - c)
    xdiag_m = (1 - x) * 2 + (1 - c)
    xpeer = {"mp": xpeer_m, "seq": s}
    cpeer = {"mp": cpeer_m, "seq": s}

    def at_z(zz):
        return {"mp": m, "seq": 2 * zz + y}

    def remote(src, dst, send, recv, dev):
        return pltpu.make_async_remote_copy(
            src_ref=src, dst_ref=dst, send_sem=send, recv_sem=recv,
            device_id=dev, device_id_type=MESH)

    def pick(a0, a1, a2, a3):
        return jnp.where(z == 0, a0, jnp.where(z == 1, a1, jnp.where(z == 2, a2, a3)))

    near = [z, pick(1, 0, 1, 2), pick(2, 2, 3, 1), pick(3, 3, 0, 0)]

    barrier = pltpu.get_barrier_semaphore()
    for d in range(1, 4):
        pl.semaphore_signal(barrier, inc=1, device_id=at_z((z + d) % 4), device_id_type=MESH)
        pl.semaphore_signal(
            barrier, inc=1, device_id={"mp": cpeer_m, "seq": 2 * ((z + d) % 4) + y}, device_id_type=MESH)
        pl.semaphore_signal(barrier, inc=1, device_id={"mp": (m + d) % 4, "seq": s}, device_id_type=MESH)
    pl.semaphore_signal(barrier, inc=1, device_id=ypeer, device_id_type=MESH)

    spans = [(0, 256), (256, 128), (384, 128)]

    def w_src(j, i):
        width = spans[i][1]
        return (wq, wk, wv)[i].at[:, pl.ds(pl.multiple_of(j * width, 128), width)]

    def wb_at(zsrc, yy, i):
        return wb.at[zsrc, pl.ds(pl.multiple_of(yy * depth, 16), depth), pl.ds(*spans[i])]

    def tb_at(k, i):
        return tb.at[k, :, pl.ds(*spans[i])]

    def c_parts(j):
        return [
            (cache_k.at[:, pl.ds(j * 128, 128)], kv.at[pl.ds(0, 1024), pl.ds(0, 128)]),
            (cache_v.at[:, pl.ds(j * 128, 128)], kv.at[pl.ds(0, 1024), pl.ds(128, 128)]),
        ]

    half = rows // 2
    full = cols // 128
    main = full * 128

    def h_src(hf):
        return hidden.at[:, pl.ds(hf * half, half)]

    own_x = [(None, pltpu.make_async_copy(h_src(hf), xb.at[z, m, hf], local_sem.at[8 + hf])) for hf in range(2)]
    own_w = [
        (m == z, pltpu.make_async_copy(w_src(m, i), wb_at(z, y, i), local_sem.at[1 + i])) for i in range(3)
    ]
    own_c = []
    for j in range(4):
        mine = (m == j) & (z == j)
        own_c.extend((mine, pltpu.make_async_copy(a, b, local_sem.at[4 + i])) for i, (a, b) in enumerate(c_parts(j)))
    own_o = [
        (None, pltpu.make_async_copy(wo.at[:, pl.ds(h * 256, 256)], ob.at[2 * y + h], local_sem.at[6 + h]))
        for h in range(2)
    ]

    def when(cond, fn):
        if cond is None:
            fn()
        else:
            pl.when(cond)(fn)

    for cond, cp in own_x + own_w + own_c + own_o:
        when(cond, cp.start)

    pl.semaphore_wait(barrier, 10)

    pending = []

    def send(cond, cp):
        when(cond, cp.start)
        pending.append((cond, cp))

    def xb_at(zz, mm, hf):
        return xb.at[zz, mm, hf]

    def x_src(zz, hf, own):
        return h_src(hf) if own else xb_at(zz, m, hf)

    def x_right(zz, hf, own=False):
        return remote(
            x_src(zz, hf, own), xb_at(zz, m, hf), xz_send.at[0, zz, hf], xz_recv.at[zz, hf], at_z((z + 1) % 4))

    def x_left(zz, hf, own=False):
        return remote(
            x_src(zz, hf, own), xb_at(zz, m, hf), xz_send.at[1, zz, hf], xz_recv.at[zz, hf], at_z((z + 3) % 4))

    def x_x(zz, hf, own=False):
        return remote(x_src(zz, hf, own), xb_at(zz, m, hf), xx_send.at[zz, hf], xx_recv.at[zz, hf], xpeer)

    def x_c(zz, hf, which, own=False):
        mm = m if which == 0 else xpeer_m
        return remote(h_src(hf) if own else xb_at(zz, mm, hf), xb_at(zz, mm, hf), xc_send.at[which, zz, hf],
                      xc_recv.at[which, zz, hf], cpeer)

    def w_cross(i, n):
        j = (xpeer_m, xdiag_m)[n]
        dev = {"mp": j, "seq": s}
        send(z == m, remote(w_src(j, i), wb_at(z, y, i), w_send.at[2 + n, i], wz_recv.at[z, i], dev))
        send(z != m, remote(w_src(j, i), tb_at(c, i), w_send.at[2 + n, i], t_recv.at[c, i], dev))

    def w_direct(i, n):
        if n == 0:
            send(m != z, remote(w_src(m, i), wb_at(z, y, i), w_send.at[0, i], wz_recv.at[z, i], at_z(m)))
        else:
            send(None, remote(w_src(cpeer_m, i), wb_at(z, y, i), w_send.at[1, i], wz_recv.at[z, i],
                              {"mp": cpeer_m, "seq": 2 * m + y}))

    def w_relay(i, n):
        cc = c if n == 0 else 1 - c
        k = (1 - x) * 2 + cc
        cp = remote(tb_at(cc, i), wb_at(z, y, i), rl_send.at[n, i], wz_recv.at[z, i], at_z(k))
        pl.when(k != z)(remote(tb_at(cc, i), tb_at(cc, i), rl_send.at[n, i], t_recv.at[cc, i], ypeer).wait_recv)
        send(k != z, cp)

    def w_along_y(n, i):
        zs = near[n]
        landed = remote(wb_at(zs, y, i), wb_at(zs, y, i), wy_send.at[n, i], wz_recv.at[zs, i], ypeer)
        if n == 0:
            pl.when(m == z)(own_w[i][1].wait)
            pl.when(m != z)(landed.wait_recv)
        else:
            landed.wait_recv()
        send(None, remote(wb_at(zs, y, i), wb_at(zs, y, i), wy_send.at[n, i], wy_recv.at[zs, i], ypeer))

    def from_left(d, hf):
        left = z - d
        lz = (z + 4 - d) % 4
        when(left >= 0, x_right(lz, hf).wait_recv)
        send((left >= 0) & (z < 3), x_right(lz, hf))
        send(left >= 0, x_x(lz, hf))
        send(left >= 0, x_c(lz, hf, 0))

    def from_right(d, hf):
        right = z + d
        rz = (z + d) % 4
        when(right <= 3, x_right(rz, hf).wait_recv)
        send((right <= 3) & (z > 0), x_left(rz, hf))
        send(right <= 3, x_x(rz, hf))
        send(right <= 3, x_c(rz, hf, 0))

    def x_cross(n, hf):
        zz = near[n]
        x_x(zz, hf).wait_recv()
        send(None, x_c(zz, hf, 1))

    def own_z(hf):
        send(z < 3, x_right(z, hf, True))
        send(z > 0, x_left(z, hf, True))

    def own_across(hf):
        send(None, x_x(z, hf, True))

    def own_core(hf):
        send(None, x_c(z, hf, 0, True))

    def o_half(h):
        send(None, remote(wo.at[:, pl.ds(h * 256, 256)], ob.at[2 * y + h], oy_send.at[h], oy_recv.at[h], ypeer))

    def cache(far):
        for j in range(4):
            for i, (a, b) in enumerate(c_parts(j)):
                send((m == z) & (m != j) & ((z < 2) if far else (z >= 2)),
                     remote(a, b, c_send.at[j, i], c_recv.at[i], {"mp": j, "seq": s}))

    def norm_block(n):
        b = near[n]
        for hf in range(2):
            for which, mm in enumerate((cpeer_m, xdiag_m)):
                remote(xb_at(b, mm, hf), xb_at(b, mm, hf), xc_send.at[which, b, hf], xc_recv.at[which, b, hf],
                       cpeer).wait_recv()
        if n == 0:
            for _, cp in own_x:
                cp.wait()

        def piece(hf, carry):
            def squares(mm, total):
                v = xb[b, mm, hf].astype(f32)
                return total + jnp.sum((v * v).reshape(cols // 32, 32, 128), axis=0)

            total = lax.fori_loop(0, NM, squares, jnp.zeros((32, 128), f32))
            scale = lax.rsqrt(jnp.sum(total, axis=0, keepdims=True) / MODEL_WIDTH + epsilon)
            scale = jnp.transpose(jnp.broadcast_to(scale, (half, 128)))
            r = pl.ds(pl.multiple_of(n * rows + hf * half, half), half)
            for t in range(NM * full + 2):
                if t < NM * full:
                    v = xb[b, t // full, hf, t % full * 128:(t % full + 1) * 128, :]
                else:
                    i = 2 * (t - NM * full)
                    v = jnp.concatenate([xb[b, i, hf, main:cols, :], xb[b, i + 1, hf, main:cols, :]], axis=0)
                v = jnp.transpose(v).astype(f32)
                xn[r, t * 128:(t + 1) * 128] = (v * scale * g_in[t:t + 1, :]).astype(bf16)
            return carry

        lax.fori_loop(0, 2, piece, 0)

    def angles(n):
        b = near[n]
        r = pl.ds(pl.multiple_of(b * rows, rows), rows)
        place = start[0] + (2 * b + y) * rows + lax.broadcasted_iota(jnp.int32, (rows, 128), 0)
        angle = place.astype(f32) * freq[...]
        lane = lax.broadcasted_iota(jnp.int32, (rows, 128), 1)
        sine = jnp.sin(angle)
        cos_t[r, :] = jnp.cos(angle)
        sin_t[r, :] = jnp.where(lane < 64, -sine, sine)

    def gains(n):
        lane = lax.broadcasted_iota(jnp.int32, (1, 128), 1)
        for mm in range(NM):
            base = mm * cols // 128
            for t in range(full):
                g = gain_in[base + t:base + t + 1, :]
                if mm % 2:
                    g = pltpu.roll(jnp.where(lane < 64, gain_in[base + t + 1:base + t + 2, :], g), 64, 1)
                g_in[mm * full + t:mm * full + t + 1, :] = g
        for i in range(2):
            low = 2 * i * cols // 128 + full
            g_in[NM * full + i:NM * full + i + 1, :] = jnp.where(
                lane < 64, gain_in[low:low + 1, :], gain_in[low + full:low + full + 1, :])
        for t in range(full + 1):
            width = min(128, cols - t * 128)
            g = jnp.broadcast_to(gain_post[t * 128:t * 128 + width][None, :], (128, width))
            g_post[t * 128:t * 128 + width, :] = jnp.transpose(g)

    def w_done(n, part):
        zs = near[n]
        for i in ((0,), (1, 2))[part]:
            landed = wb_at(zs, 1 - y, i)
            remote(landed, landed, wy_send.at[n, i], wy_recv.at[zs, i], ypeer).wait_recv()

    def w_ends(part):
        for mm in range(NM):
            wrem[mm * 64:(mm + 1) * 64, part * 256:(part + 1) * 256] = wb[mm, main:cols, part * 256:(part + 1) * 256]

    def o_done(h):
        o_in = ob.at[2 * (1 - y) + h]
        remote(o_in, o_in, oy_send.at[h], oy_recv.at[h], ypeer).wait_recv()
        own_o[h][1].wait()

    def c_done(far):
        mine = (z < 2) if far else (z >= 2)
        for i, (a, b) in enumerate(c_parts(0)):
            pl.when(mine & (m == z))(pltpu.make_async_copy(a, b, local_sem.at[4 + i]).wait)
            pl.when(mine & (m != z))(remote(b, b, c_send.at[0, i], c_recv.at[i], ypeer).wait_recv)

    def kv_copy(b):
        r = pl.ds(pl.multiple_of(1024 + (2 * b + y) * 256, 256), 256)
        return remote(kv.at[r, :], kv.at[r, :], kv_send.at[b], kv_recv.at[b], ypeer)

    def head_norm(g, gain, cosine, sine):
        g = g * lax.rsqrt(jnp.mean(g * g, axis=-1, keepdims=True) + epsilon) * gain
        return g * cosine + pltpu.roll(g, 64, 1) * sine

    def product(lo, hi, part):
        c = slice(part * 256, (part + 1) * 256)
        r = slice(lo * rows, hi * rows)
        acc = jnp.dot(xn[r, NM * main:NM * cols], wrem[:, c], preferred_element_type=f32)
        for mm in range(NM):
            acc += jnp.dot(xn[r, mm * main:(mm + 1) * main], wb[mm, 0:main, c], preferred_element_type=f32)
        return acc

    def project_q(lo, hi):
        acc = product(lo, hi, 0)
        for n in range(lo, hi):
            r = pl.ds(pl.multiple_of(near[n] * rows, rows), rows)
            cosine, sine = cos_t[r, :], sin_t[r, :]
            for h in range(2):
                q = acc[(n - lo) * rows:(n - lo + 1) * rows, h * 128:(h + 1) * 128]
                q = head_norm(q, gain_q[...], cosine, sine) * query_scale
                qb[h, r, :] = q.astype(bf16)

    def project_kv(lo, hi):
        acc = product(lo, hi, 1)
        for n in range(lo, hi):
            b = near[n]
            r = pl.ds(pl.multiple_of(b * rows, rows), rows)
            rk = pl.ds(pl.multiple_of(1024 + (2 * b + y) * 256, 256), 256)
            part = acc[(n - lo) * rows:(n - lo + 1) * rows, :]
            kv[rk, 0:128] = head_norm(part[:, 0:128], gain_k[...], cos_t[r, :], sin_t[r, :]).astype(bf16)
            kv[rk, 128:256] = part[:, 128:256].astype(bf16)
            send(None, kv_copy(b))

    def kv_done(n):
        b = near[n]
        r = pl.ds(pl.multiple_of(1024 + (2 * b + (1 - y)) * 256, 256), 256)
        remote(kv.at[r, :], kv.at[r, :], kv_send.at[b], kv_recv.at[b], ypeer).wait_recv()

    def a_copy(b, d, h):
        r = pl.ds(pl.multiple_of(b * rows, rows), rows)
        piece = ab.at[m, r, pl.ds(h * 128, 128)]
        return remote(piece, piece, a_send.at[b, d, h], a_recv.at[b, m, h], {"mp": (m + d) % 4, "seq": s})

    span = WINDOW_LENGTH + 256
    qi = lax.broadcasted_iota(jnp.int32, (rows, span), 0)
    ei = lax.broadcasted_iota(jnp.int32, (rows, span), 1)
    visible = (ei > qi) & (ei <= qi + WINDOW_LENGTH)
    order = [pick(3, 3, 0, 0), pick(2, 0, 3, 1), pick(1, 2, 1, 2), z]
    edge = (z == 0) | (z == 3)

    def attend(k, h):
        b = order[k]
        r = pl.ds(pl.multiple_of(b * rows, rows), rows)
        rk = pl.ds(pl.multiple_of((2 * b + y) * 256, 256), span)
        keys = kv[rk, 0:128]
        vals = kv[rk, 128:256]
        sc = lax.dot_general(qb[h, r, :], keys, (((1,), (1,)), ((), ())), preferred_element_type=f32)
        sc = jnp.where(visible, sc, -jnp.inf)
        top = jnp.max(sc, axis=-1, keepdims=True)
        p = jnp.exp(sc - top)
        tot = jnp.sum(p, axis=-1, keepdims=True)
        o = jnp.dot(p.astype(bf16), vals, preferred_element_type=f32)
        ab[m, r, h * 128:(h + 1) * 128] = (o / tot).astype(bf16)
        for d in (2, 3, 1):
            send(None, a_copy(b, d, h))

    def a_wait(b):
        r = pl.ds(pl.multiple_of(b * rows, rows), rows)
        for h in range(2):
            for d in range(1, 4):
                mm = (m + d) % 4
                piece = ab.at[mm, r, pl.ds(h * 128, 128)]
                remote(piece, piece, a_send.at[b, d, h], a_recv.at[b, mm, h], ypeer).wait_recv()

    def partial(b):
        r = pl.ds(pl.multiple_of(b * rows, rows), rows)
        acc = None
        for mm in range(NM):
            term = lax.dot_general(ob[mm], ab[mm, r, :], (((1,), (1,)), ((), ())), preferred_element_type=f32)
            acc = term if acc is None else acc + term
        for hf in range(2):
            pacc[hf] = acc[:, hf * half:(hf + 1) * half]

    def r_copy(side, b, hf, zd):
        return remote(sb.at[b, hf], rb.at[side, b, hf], r_send.at[b, hf], r_recv.at[side, b, hf], at_z(zd))

    def hop(b):
        right = b > z
        side = jnp.where(right, 0, 1)
        target = jnp.where(right, (z + 1) % 4, (z + 3) % 4)
        inner = (right & (z > 0)) | (jnp.logical_not(right) & (z < 3))
        partial(b)
        for hf in range(2):
            @pl.when(inner)
            def _():
                r_copy(side, b, hf, target).wait_recv()
                sb[b, hf] = (pacc[hf] + rb[side, b, hf].astype(f32)).astype(bf16)

            @pl.when(jnp.logical_not(inner))
            def _():
                sb[b, hf] = pacc[hf].astype(bf16)

            r_copy(side, b, hf, target).start()

    def hop_step(k):
        a_wait(order[k])
        hop(order[k])

    def hop_edge(k):
        pl.when(edge)(lambda: hop_step(k))

    def hop_inner(k):
        pl.when(jnp.logical_not(edge))(lambda: hop_step(k))

    steps = {
        "xz": own_z, "xx": own_across, "xc": own_core, "wc": w_cross, "wd": w_direct, "wo": o_half, "wr": w_relay,
        "wy": w_along_y, "xl": from_left, "xr": from_right, "xk": x_cross, "ca": cache, "nm": norm_block,
        "we": w_done, "wm": w_ends, "od": o_done, "cd": c_done, "pq": project_q, "pk": project_kv, "kd": kv_done,
        "tr": angles, "gp": gains, "at": attend, "he": hop_edge, "hi": hop_inner, "hp": hop_step,
    }
    for name, *rest in SCHEDULE:
        steps[name](*rest)

    a_wait(order[3])

    partial(z)

    def add_arrived(side, hf):
        r_copy(side, z, hf, z).wait_recv()
        pacc[hf] += rb[side, z, hf].astype(f32)

    for hf in range(2):
        pl.when(z > 0)(functools.partial(add_arrived, 0, hf))
        pl.when(z < 3)(functools.partial(add_arrived, 1, hf))
        mixed = pacc[hf]
        squares = jnp.sum(mixed * mixed, axis=0, keepdims=True)
        ss[m, :, hf * half:(hf + 1) * half] = jnp.broadcast_to(squares, (8, half))

    def s_copy(d):
        return remote(ss.at[m], ss.at[m], s_send.at[d], s_recv.at[m], {"mp": (m + d) % 4, "seq": s})

    for d in range(1, 4):
        s_copy(d).start()
    for d in range(1, 4):
        mm = (m + d) % 4
        remote(ss.at[mm], ss.at[mm], s_send.at[d], s_recv.at[mm], ypeer).wait_recv()
    squares = (ss[0] + ss[1] + ss[2] + ss[3])[0:1, :]
    scaling = lax.rsqrt(squares / MODEL_WIDTH + epsilon)
    for hf in range(2):
        part = slice(hf * half, (hf + 1) * half)
        out[:, part] = (xb[z, m, hf].astype(f32) + pacc[hf] * scaling[:, part] * g_post[...]).astype(bf16)

    for d in range(1, 4):
        s_copy(d).wait_send()
    for d in range(4):
        for hf in range(2):
            when(z != d, r_copy(0, d, hf, (z + 1) % 4).wait_send)
    for cond, cp in pending:
        when(cond, cp.wait_send)


def fused(
    hidden_in, gain_in, w_query, key_weight, value_weight, gain_query, gain_key, start_pos,
    cached_key_rows, cached_value_rows, w_out, gain_post,
):
    rows, cols = hidden_in.shape
    depth = w_query.shape[0]
    inverse_freq = rope_base ** (-(np.arange(64) * 2.0) / 128)
    freq = jnp.asarray(np.concatenate([inverse_freq, inverse_freq])[None, :], f32)
    hbm = pl.BlockSpec(memory_space=pl.ANY)
    vmem = pl.BlockSpec(memory_space=pltpu.VMEM)
    smem = pl.BlockSpec(memory_space=pltpu.SMEM)
    dma = pltpu.SemaphoreType.DMA
    turned = pl.pallas_call(
        layer_kernel,
        name="layer",
        out_shape=pltpu.VMEM((cols, rows), bf16),
        in_specs=[hbm, vmem, hbm, hbm, hbm, vmem, vmem, smem, vmem, hbm, hbm, hbm, vmem],
        out_specs=vmem,
        scratch_shapes=[
            pltpu.VMEM((1024, 128), f32),
            pltpu.VMEM((1024, 128), f32),
            pltpu.VMEM((4 * cols // 128, 128), f32),
            pltpu.VMEM((cols, 128), f32),
            pltpu.VMEM((4, 4, 2, cols, 128), bf16),
            pltpu.VMEM((4 * rows, 4 * cols), bf16),
            pltpu.VMEM((2, depth, 512), bf16),
            pltpu.VMEM((4, 2 * depth, 512), bf16),
            pltpu.VMEM((256, 512), bf16),
            pltpu.VMEM((4, cols, 256), bf16),
            pltpu.VMEM((3072, 256), bf16),
            pltpu.VMEM((2, 1024, 128), bf16),
            pltpu.VMEM((4, 1024, 256), bf16),
            pltpu.VMEM((2, 4, 2, cols, 128), bf16),
            pltpu.VMEM((4, 2, cols, 128), bf16),
            pltpu.VMEM((4, 8, rows), f32),
            pltpu.VMEM((2, cols, 128), f32),
            dma((10,)), dma((2, 4, 2)), dma((4, 2)), dma((4, 2)), dma((4, 2)), dma((2, 4, 2)), dma((2, 4, 2)),
            dma((4, 3)), dma((2, 3)), dma((2, 3)), dma((4, 3)), dma((4, 3)), dma((4, 3)), dma((4, 2)), dma((2,)), dma((2,)), dma((2,)),
            dma((4,)), dma((4,)), dma((4, 4, 2)), dma((4, 4, 2)), dma((4, 2)), dma((2, 4, 2)), dma((4,)), dma((4,)),
        ],
        compiler_params=pltpu.CompilerParams(
            collective_id=0, has_side_effects=True, vmem_limit_bytes=60 * 1024 * 1024,
        ),
    )(
        hidden_in.T, gain_in.reshape(-1, 128), w_query, key_weight, value_weight,
        gain_query.reshape(1, 128), gain_key.reshape(1, 128), start_pos, freq,
        cached_key_rows, cached_value_rows, w_out.T, gain_post,
    )
    return turned.T


def shifted(x, axis, by):
    peers = lax.axis_size(axis)
    pairs = [(i, i + by) for i in range(peers) if 0 <= i + by < peers]
    return lax.ppermute(x, axis, pairs)


def norm_rows(values, gain):
    return values * lax.rsqrt(jnp.mean(values * values, axis=-1, keepdims=True) + epsilon) * gain


def rotate(tensor, positions):
    half_dim = tensor.shape[-1] // 2
    inverse_freq = rope_base ** (
        -(jnp.arange(half_dim, dtype=jnp.float32) * 2.0) / tensor.shape[-1]
    )
    angles = positions.astype(jnp.float32)[:, None, None] * inverse_freq[None, None, :]
    cosine = jnp.cos(angles)
    sine = jnp.sin(angles)
    first = tensor[..., :half_dim]
    second = tensor[..., half_dim:]
    return jnp.concatenate(
        [first * cosine - second * sine, second * cosine + first * sine], axis=-1
    )


def on_device(
    hidden_in,
    gain_in,
    w_query,
    key_weight,
    value_weight,
    gain_query,
    gain_key,
    start_pos,
    cached_key_rows,
    cached_value_rows,
    w_out,
    gain_post,
):
    n_rows = hidden_in.shape[0]
    head_dim = gain_query.shape[0]
    kv_cols = key_weight.shape[1]
    kv_heads = kv_cols // head_dim
    q_heads = w_query.shape[1] // head_dim
    query_group_count = q_heads // kv_heads
    full_rows = lax.all_gather(hidden_in, "mp", axis=1, tiled=True)
    normed_hidden = norm_rows(full_rows.astype(jnp.float32), gain_in).astype(jnp.bfloat16)

    def add_rows(block_rows):
        return jnp.dot(normed_hidden, block_rows, preferred_element_type=jnp.float32)

    keys_raw = add_rows(lax.all_gather(key_weight, "seq", axis=0, tiled=True))
    values_raw = add_rows(lax.all_gather(value_weight, "seq", axis=0, tiled=True))
    query_matrix = add_rows(lax.all_gather(w_query, "seq", axis=0, tiled=True))
    seq_index = lax.axis_index("seq")
    positions = start_pos[0] + seq_index * n_rows + jnp.arange(n_rows, dtype=jnp.int32)
    query_matrix = (
        rotate(norm_rows(query_matrix.reshape(n_rows, q_heads, head_dim), gain_query), positions)
        * query_scale
    ).astype(jnp.bfloat16)
    fresh_key = rotate(
        norm_rows(keys_raw.reshape(n_rows, kv_heads, head_dim), gain_key), positions
    ).astype(jnp.bfloat16)
    fresh = jnp.stack([fresh_key.reshape(n_rows, kv_cols), values_raw.astype(jnp.bfloat16)])
    reach_shards = (WINDOW_LENGTH + n_rows - 1) // n_rows
    reach_rows = reach_shards * n_rows
    pieces = []
    moving = fresh
    for hop_index in range(reach_shards):
        moving = shifted(moving, "seq", 1)
        pieces.insert(0, moving)
    prior = jnp.concatenate(pieces, axis=1)
    front_pad = reach_rows - WINDOW_LENGTH
    cached = jnp.stack([cached_key_rows, cached_value_rows])
    padded = jnp.concatenate(
        [
            jnp.zeros((2, front_pad, kv_cols), cached.dtype),
            cached,
            jnp.zeros((2, reach_rows, kv_cols), cached.dtype),
        ],
        axis=1,
    )
    cache_start = jnp.minimum(seq_index * n_rows, front_pad + WINDOW_LENGTH)
    from_cache = lax.dynamic_slice_in_dim(padded, cache_start, reach_rows, 1)
    prior_rows = jnp.arange(reach_rows, dtype=jnp.int32)
    use_cache = prior_rows < reach_rows - seq_index * n_rows
    prior = jnp.where(use_cache[None, :, None], from_cache, prior)
    window_kv = jnp.concatenate([prior, fresh], axis=1)
    span_rows = reach_rows + n_rows
    key_heads = window_kv[0].reshape(span_rows, kv_heads, head_dim)
    value_heads = window_kv[1].reshape(span_rows, kv_heads, head_dim)
    query_heads = query_matrix.reshape(n_rows, kv_heads, query_group_count, head_dim)
    scores = jnp.einsum(
        "tkgd,skd->kgts", query_heads, key_heads, preferred_element_type=jnp.float32
    )
    query_index = jnp.arange(n_rows, dtype=jnp.int32)[:, None]
    key_index = jnp.arange(span_rows, dtype=jnp.int32)[None, :]
    visible = (key_index > query_index + reach_rows - WINDOW_LENGTH) & (
        key_index <= query_index + reach_rows
    )
    scores = jnp.where(visible, scores, -jnp.inf)
    row_max = jnp.max(scores, axis=-1, keepdims=True)
    probs = jnp.exp(scores - row_max)
    totals = jnp.sum(probs, axis=-1)
    probs_b = probs.astype(jnp.bfloat16)
    summed = jnp.einsum("kgts,skd->tkgd", probs_b, value_heads, preferred_element_type=jnp.float32)
    summed = summed / jnp.transpose(totals, (2, 0, 1))[..., None]
    attn = summed.reshape(n_rows, q_heads * head_dim).astype(jnp.bfloat16)
    all_heads = lax.all_gather(attn, "mp", axis=1, tiled=True)
    projected = jnp.dot(
        all_heads,
        lax.all_gather(w_out, "seq", axis=0, tiled=True),
        preferred_element_type=jnp.float32,
    )
    squares = lax.psum(jnp.sum(projected * projected, axis=-1), "mp")
    scaling = lax.rsqrt(squares / MODEL_WIDTH + epsilon)
    return (hidden_in.astype(jnp.float32) + projected * scaling[:, None] * gain_post).astype(
        jnp.bfloat16
    )


def solution(mesh):
    in_specs = (
        P("seq", "mp"),
        P(),
        P("seq", "mp"),
        P("seq", "mp"),
        P("seq", "mp"),
        P(),
        P(),
        P(),
        P(None, "mp"),
        P(None, "mp"),
        P("seq", "mp"),
        P("mp"),
    )
    out_specs = P("seq", "mp")
    fits = mesh.shape["mp"] == 4 and mesh.shape["seq"] == 8
    return jax.shard_map(
        fused if fits else on_device, mesh=mesh, in_specs=in_specs, out_specs=out_specs, check_vma=False
    )
```

```python
import functools

import jax
import jax.numpy as jnp
import numpy as np
from jax import lax
from jax.experimental import pallas as pl
from jax.experimental.pallas import tpu as pltpu
from jax.sharding import PartitionSpec as P

MODEL_WIDTH = 5376
WINDOW_LENGTH = 1024


epsilon = 1e-06
query_scale = 168.0 ** (-0.5)
rope_base = 10000.0

MESH = pl.DeviceIdType.MESH
f32 = jnp.float32
bf16 = jnp.bfloat16


SCHEDULE = (
    ("wc", 0, 0), ("wo", 1), ("xz", 0), ("wc", 0, 1), ("wc", 2, 0), ("xz", 1), ("wc", 1, 0), ("gp", 0),
    ("xl", 1, 0), ("xr", 1, 0), ("wy", 0, 0), ("xx", 0), ("wd", 0, 0), ("tr", 0), ("wc", 2, 1), ("wc", 1, 1),
    ("wr", 0, 0), ("tr", 2), ("wr", 0, 1), ("xl", 1, 1), ("wo", 0), ("xx", 1), ("xr", 1, 1), ("wd", 0, 1),
    ("wy", 0, 1), ("xc", 0), ("wy", 0, 2), ("xl", 2, 0), ("wr", 2, 0), ("xk", 0, 0), ("tr", 3), ("xr", 2, 0),
    ("wy", 3, 0), ("wd", 2, 0), ("wr", 2, 1), ("wy", 1, 0), ("wd", 2, 1), ("wd", 1, 1), ("tr", 1), ("we", 3, 0),
    ("wy", 2, 0), ("od", 1), ("xk", 1, 1), ("wr", 1, 1), ("xr", 2, 1), ("xk", 1, 0), ("xl", 2, 1), ("wy", 1, 2),
    ("xk", 2, 0), ("od", 0), ("xr", 3, 0), ("wy", 3, 2), ("xl", 3, 0), ("xk", 2, 1), ("wy", 2, 2), ("nm", 1),
    ("xk", 0, 1), ("xk", 3, 0), ("wr", 1, 0), ("xl", 3, 1), ("xr", 3, 1), ("wd", 1, 0), ("we", 0, 0),
    ("wy", 1, 1), ("xc", 1), ("we", 0, 1), ("nm", 2), ("wy", 3, 1), ("we", 2, 0), ("wy", 2, 1), ("we", 1, 1),
    ("ca", 1), ("xk", 3, 1), ("ca", 0), ("we", 1, 0), ("wm", 0), ("nm", 0), ("we", 2, 1), ("we", 3, 1),
    ("wm", 1), ("pk", 0, 3), ("nm", 3), ("pk", 3, 4), ("cd", 0), ("pq", 3, 4), ("kd", 0), ("kd", 1), ("kd", 2),
    ("kd", 3), ("at", 0, 0), ("at", 0, 1), ("he", 0), ("pq", 0, 3), ("cd", 1), ("at", 1, 0), ("at", 1, 1),
    ("hi", 0), ("at", 2, 1), ("at", 2, 0), ("hp", 1), ("hp", 2), ("at", 3, 0), ("at", 3, 1),
)


def layer_kernel(
    hidden, gain_in, wq, wk, wv, gain_q, gain_k, start, freq, cache_k, cache_v, wo, gain_post,
    out,
    cos_t, sin_t, g_in, g_post, xb, xn, tb, wb, wrem, ob, kv, qb, ab, rb, sb, ss, pacc,
    local_sem, xz_send, xz_recv, xx_send, xx_recv, xc_send, xc_recv,
    w_send, t_recv, rl_send, wz_recv, wy_send, wy_recv, c_send, c_recv, oy_send, oy_recv,
    kv_send, kv_recv, a_send, a_recv, r_send, r_recv, s_send, s_recv,
):
    NZ, NM = 4, 4
    cols, rows = hidden.shape
    depth = wq.shape[0]
    m = lax.axis_index("mp")
    s = lax.axis_index("seq")
    z, y = s // 2, s % 2
    x, c = m // 2, m % 2
    ypeer = {"mp": m, "seq": 2 * z + (1 - y)}
    xpeer_m = (1 - x) * 2 + c
    cpeer_m = x * 2 + (1 - c)
    xdiag_m = (1 - x) * 2 + (1 - c)
    xpeer = {"mp": xpeer_m, "seq": s}
    cpeer = {"mp": cpeer_m, "seq": s}

    def at_z(zz):
        return {"mp": m, "seq": 2 * zz + y}

    def remote(src, dst, send, recv, dev):
        return pltpu.make_async_remote_copy(
            src_ref=src, dst_ref=dst, send_sem=send, recv_sem=recv,
            device_id=dev, device_id_type=MESH)

    def pick(a0, a1, a2, a3):
        return jnp.where(z == 0, a0, jnp.where(z == 1, a1, jnp.where(z == 2, a2, a3)))

    near = [z, pick(1, 0, 1, 2), pick(2, 2, 3, 1), pick(3, 3, 0, 0)]

    barrier = pltpu.get_barrier_semaphore()
    for d in range(1, 4):
        pl.semaphore_signal(barrier, inc=1, device_id=at_z((z + d) % 4), device_id_type=MESH)
        pl.semaphore_signal(
            barrier, inc=1, device_id={"mp": cpeer_m, "seq": 2 * ((z + d) % 4) + y}, device_id_type=MESH)
        pl.semaphore_signal(barrier, inc=1, device_id={"mp": (m + d) % 4, "seq": s}, device_id_type=MESH)
    pl.semaphore_signal(barrier, inc=1, device_id=ypeer, device_id_type=MESH)

    spans = [(0, 256), (256, 128), (384, 128)]

    def w_src(j, i):
        width = spans[i][1]
        return (wq, wk, wv)[i].at[:, pl.ds(pl.multiple_of(j * width, 128), width)]

    def wb_at(zsrc, yy, i):
        return wb.at[zsrc, pl.ds(pl.multiple_of(yy * depth, 16), depth), pl.ds(*spans[i])]

    def tb_at(k, i):
        return tb.at[k, :, pl.ds(*spans[i])]

    def c_parts(j):
        return [
            (cache_k.at[:, pl.ds(j * 128, 128)], kv.at[pl.ds(0, 1024), pl.ds(0, 128)]),
            (cache_v.at[:, pl.ds(j * 128, 128)], kv.at[pl.ds(0, 1024), pl.ds(128, 128)]),
        ]

    half = rows // 2
    full = cols // 128
    main = full * 128

    def h_src(hf):
        return hidden.at[:, pl.ds(hf * half, half)]

    own_x = [(None, pltpu.make_async_copy(h_src(hf), xb.at[z, m, hf], local_sem.at[8 + hf])) for hf in range(2)]
    own_w = [
        (m == z, pltpu.make_async_copy(w_src(m, i), wb_at(z, y, i), local_sem.at[1 + i])) for i in range(3)
    ]
    own_c = []
    for j in range(4):
        mine = (m == j) & (z == j)
        own_c.extend((mine, pltpu.make_async_copy(a, b, local_sem.at[4 + i])) for i, (a, b) in enumerate(c_parts(j)))
    own_o = [
        (None, pltpu.make_async_copy(wo.at[:, pl.ds(h * 256, 256)], ob.at[2 * y + h], local_sem.at[6 + h]))
        for h in range(2)
    ]

    def when(cond, fn):
        if cond is None:
            fn()
        else:
            pl.when(cond)(fn)

    for cond, cp in own_x + own_w + own_c + own_o:
        when(cond, cp.start)

    pl.semaphore_wait(barrier, 10)

    pending = []

    def send(cond, cp):
        when(cond, cp.start)
        pending.append((cond, cp))

    def xb_at(zz, mm, hf):
        return xb.at[zz, mm, hf]

    def x_src(zz, hf, own):
        return h_src(hf) if own else xb_at(zz, m, hf)

    def x_right(zz, hf, own=False):
        return remote(
            x_src(zz, hf, own), xb_at(zz, m, hf), xz_send.at[0, zz, hf], xz_recv.at[zz, hf], at_z((z + 1) % 4))

    def x_left(zz, hf, own=False):
        return remote(
            x_src(zz, hf, own), xb_at(zz, m, hf), xz_send.at[1, zz, hf], xz_recv.at[zz, hf], at_z((z + 3) % 4))

    def x_x(zz, hf, own=False):
        return remote(x_src(zz, hf, own), xb_at(zz, m, hf), xx_send.at[zz, hf], xx_recv.at[zz, hf], xpeer)

    def x_c(zz, hf, which, own=False):
        mm = m if which == 0 else xpeer_m
        return remote(h_src(hf) if own else xb_at(zz, mm, hf), xb_at(zz, mm, hf), xc_send.at[which, zz, hf],
                      xc_recv.at[which, zz, hf], cpeer)

    def w_cross(i, n):
        j = (xpeer_m, xdiag_m)[n]
        dev = {"mp": j, "seq": s}
        send(z == m, remote(w_src(j, i), wb_at(z, y, i), w_send.at[2 + n, i], wz_recv.at[z, i], dev))
        send(z != m, remote(w_src(j, i), tb_at(c, i), w_send.at[2 + n, i], t_recv.at[c, i], dev))

    def w_direct(i, n):
        if n == 0:
            send(m != z, remote(w_src(m, i), wb_at(z, y, i), w_send.at[0, i], wz_recv.at[z, i], at_z(m)))
        else:
            send(None, remote(w_src(cpeer_m, i), wb_at(z, y, i), w_send.at[1, i], wz_recv.at[z, i],
                              {"mp": cpeer_m, "seq": 2 * m + y}))

    def w_relay(i, n):
        cc = c if n == 0 else 1 - c
        k = (1 - x) * 2 + cc
        cp = remote(tb_at(cc, i), wb_at(z, y, i), rl_send.at[n, i], wz_recv.at[z, i], at_z(k))
        pl.when(k != z)(remote(tb_at(cc, i), tb_at(cc, i), rl_send.at[n, i], t_recv.at[cc, i], ypeer).wait_recv)
        send(k != z, cp)

    def w_along_y(n, i):
        zs = near[n]
        landed = remote(wb_at(zs, y, i), wb_at(zs, y, i), wy_send.at[n, i], wz_recv.at[zs, i], ypeer)
        if n == 0:
            pl.when(m == z)(own_w[i][1].wait)
            pl.when(m != z)(landed.wait_recv)
        else:
            landed.wait_recv()
        send(None, remote(wb_at(zs, y, i), wb_at(zs, y, i), wy_send.at[n, i], wy_recv.at[zs, i], ypeer))

    def from_left(d, hf):
        left = z - d
        lz = (z + 4 - d) % 4
        when(left >= 0, x_right(lz, hf).wait_recv)
        send((left >= 0) & (z < 3), x_right(lz, hf))
        send(left >= 0, x_x(lz, hf))
        send(left >= 0, x_c(lz, hf, 0))

    def from_right(d, hf):
        right = z + d
        rz = (z + d) % 4
        when(right <= 3, x_right(rz, hf).wait_recv)
        send((right <= 3) & (z > 0), x_left(rz, hf))
        send(right <= 3, x_x(rz, hf))
        send(right <= 3, x_c(rz, hf, 0))

    def x_cross(n, hf):
        zz = near[n]
        x_x(zz, hf).wait_recv()
        send(None, x_c(zz, hf, 1))

    def own_z(hf):
        send(z < 3, x_right(z, hf, True))
        send(z > 0, x_left(z, hf, True))

    def own_across(hf):
        send(None, x_x(z, hf, True))

    def own_core(hf):
        send(None, x_c(z, hf, 0, True))

    def o_half(h):
        send(None, remote(wo.at[:, pl.ds(h * 256, 256)], ob.at[2 * y + h], oy_send.at[h], oy_recv.at[h], ypeer))

    def cache(far):
        for j in range(4):
            for i, (a, b) in enumerate(c_parts(j)):
                send((m == z) & (m != j) & ((z < 2) if far else (z >= 2)),
                     remote(a, b, c_send.at[j, i], c_recv.at[i], {"mp": j, "seq": s}))

    def norm_block(n):
        b = near[n]
        for hf in range(2):
            for which, mm in enumerate((cpeer_m, xdiag_m)):
                remote(xb_at(b, mm, hf), xb_at(b, mm, hf), xc_send.at[which, b, hf], xc_recv.at[which, b, hf],
                       cpeer).wait_recv()
        if n == 0:
            for _, cp in own_x:
                cp.wait()

        def piece(hf, carry):
            def squares(mm, total):
                v = xb[b, mm, hf].astype(f32)
                return total + jnp.sum((v * v).reshape(cols // 32, 32, 128), axis=0)

            total = lax.fori_loop(0, NM, squares, jnp.zeros((32, 128), f32))
            scale = lax.rsqrt(jnp.sum(total, axis=0, keepdims=True) / MODEL_WIDTH + epsilon)
            scale = jnp.transpose(jnp.broadcast_to(scale, (half, 128)))
            r = pl.ds(pl.multiple_of(n * rows + hf * half, half), half)
            for t in range(NM * full + 2):
                if t < NM * full:
                    v = xb[b, t // full, hf, t % full * 128:(t % full + 1) * 128, :]
                else:
                    i = 2 * (t - NM * full)
                    v = jnp.concatenate([xb[b, i, hf, main:cols, :], xb[b, i + 1, hf, main:cols, :]], axis=0)
                v = jnp.transpose(v).astype(f32)
                xn[r, t * 128:(t + 1) * 128] = (v * scale * g_in[t:t + 1, :]).astype(bf16)
            return carry

        lax.fori_loop(0, 2, piece, 0)

    def angles(n):
        b = near[n]
        r = pl.ds(pl.multiple_of(b * rows, rows), rows)
        place = start[0] + (2 * b + y) * rows + lax.broadcasted_iota(jnp.int32, (rows, 128), 0)
        angle = place.astype(f32) * freq[...]
        lane = lax.broadcasted_iota(jnp.int32, (rows, 128), 1)
        sine = jnp.sin(angle)
        cos_t[r, :] = jnp.cos(angle)
        sin_t[r, :] = jnp.where(lane < 64, -sine, sine)

    def gains(n):
        lane = lax.broadcasted_iota(jnp.int32, (1, 128), 1)
        for mm in range(NM):
            base = mm * cols // 128
            for t in range(full):
                g = gain_in[base + t:base + t + 1, :]
                if mm % 2:
                    g = pltpu.roll(jnp.where(lane < 64, gain_in[base + t + 1:base + t + 2, :], g), 64, 1)
                g_in[mm * full + t:mm * full + t + 1, :] = g
        for i in range(2):
            low = 2 * i * cols // 128 + full
            g_in[NM * full + i:NM * full + i + 1, :] = jnp.where(
                lane < 64, gain_in[low:low + 1, :], gain_in[low + full:low + full + 1, :])
        for t in range(full + 1):
            width = min(128, cols - t * 128)
            g = jnp.broadcast_to(gain_post[t * 128:t * 128 + width][None, :], (128, width))
            g_post[t * 128:t * 128 + width, :] = jnp.transpose(g)

    def w_done(n, part):
        zs = near[n]
        for i in ((0,), (1, 2))[part]:
            landed = wb_at(zs, 1 - y, i)
            remote(landed, landed, wy_send.at[n, i], wy_recv.at[zs, i], ypeer).wait_recv()

    def w_ends(part):
        for mm in range(NM):
            wrem[mm * 64:(mm + 1) * 64, part * 256:(part + 1) * 256] = wb[mm, main:cols, part * 256:(part + 1) * 256]

    def o_done(h):
        o_in = ob.at[2 * (1 - y) + h]
        remote(o_in, o_in, oy_send.at[h], oy_recv.at[h], ypeer).wait_recv()
        own_o[h][1].wait()

    def c_done(far):
        mine = (z < 2) if far else (z >= 2)
        for i, (a, b) in enumerate(c_parts(0)):
            pl.when(mine & (m == z))(pltpu.make_async_copy(a, b, local_sem.at[4 + i]).wait)
            pl.when(mine & (m != z))(remote(b, b, c_send.at[0, i], c_recv.at[i], ypeer).wait_recv)

    def kv_copy(b):
        r = pl.ds(pl.multiple_of(1024 + (2 * b + y) * 256, 256), 256)
        return remote(kv.at[r, :], kv.at[r, :], kv_send.at[b], kv_recv.at[b], ypeer)

    def head_norm(g, gain, cosine, sine):
        g = g * lax.rsqrt(jnp.mean(g * g, axis=-1, keepdims=True) + epsilon) * gain
        return g * cosine + pltpu.roll(g, 64, 1) * sine

    def product(lo, hi, part):
        c = slice(part * 256, (part + 1) * 256)
        r = slice(lo * rows, hi * rows)
        acc = jnp.dot(xn[r, NM * main:NM * cols], wrem[:, c], preferred_element_type=f32)
        for mm in range(NM):
            acc += jnp.dot(xn[r, mm * main:(mm + 1) * main], wb[mm, 0:main, c], preferred_element_type=f32)
        return acc

    def project_q(lo, hi):
        acc = product(lo, hi, 0)
        for n in range(lo, hi):
            r = pl.ds(pl.multiple_of(near[n] * rows, rows), rows)
            cosine, sine = cos_t[r, :], sin_t[r, :]
            for h in range(2):
                q = acc[(n - lo) * rows:(n - lo + 1) * rows, h * 128:(h + 1) * 128]
                q = head_norm(q, gain_q[...], cosine, sine) * query_scale
                qb[h, r, :] = q.astype(bf16)

    def project_kv(lo, hi):
        acc = product(lo, hi, 1)
        for n in range(lo, hi):
            b = near[n]
            r = pl.ds(pl.multiple_of(b * rows, rows), rows)
            rk = pl.ds(pl.multiple_of(1024 + (2 * b + y) * 256, 256), 256)
            part = acc[(n - lo) * rows:(n - lo + 1) * rows, :]
            kv[rk, 0:128] = head_norm(part[:, 0:128], gain_k[...], cos_t[r, :], sin_t[r, :]).astype(bf16)
            kv[rk, 128:256] = part[:, 128:256].astype(bf16)
            send(None, kv_copy(b))

    def kv_done(n):
        b = near[n]
        r = pl.ds(pl.multiple_of(1024 + (2 * b + (1 - y)) * 256, 256), 256)
        remote(kv.at[r, :], kv.at[r, :], kv_send.at[b], kv_recv.at[b], ypeer).wait_recv()

    def a_copy(b, d, h):
        r = pl.ds(pl.multiple_of(b * rows, rows), rows)
        piece = ab.at[m, r, pl.ds(h * 128, 128)]
        return remote(piece, piece, a_send.at[b, d, h], a_recv.at[b, m, h], {"mp": (m + d) % 4, "seq": s})

    span = WINDOW_LENGTH + 256
    qi = lax.broadcasted_iota(jnp.int32, (rows, span), 0)
    ei = lax.broadcasted_iota(jnp.int32, (rows, span), 1)
    visible = (ei > qi) & (ei <= qi + WINDOW_LENGTH)
    order = [pick(3, 3, 0, 0), pick(2, 0, 3, 1), pick(1, 2, 1, 2), z]
    edge = (z == 0) | (z == 3)

    def attend(k, h):
        b = order[k]
        r = pl.ds(pl.multiple_of(b * rows, rows), rows)
        rk = pl.ds(pl.multiple_of((2 * b + y) * 256, 256), span)
        keys = kv[rk, 0:128]
        vals = kv[rk, 128:256]
        sc = lax.dot_general(qb[h, r, :], keys, (((1,), (1,)), ((), ())), preferred_element_type=f32)
        sc = jnp.where(visible, sc, -jnp.inf)
        top = jnp.max(sc, axis=-1, keepdims=True)
        p = jnp.exp(sc - top)
        tot = jnp.sum(p, axis=-1, keepdims=True)
        o = jnp.dot(p.astype(bf16), vals, preferred_element_type=f32)
        ab[m, r, h * 128:(h + 1) * 128] = (o / tot).astype(bf16)
        for d in (2, 3, 1):
            send(None, a_copy(b, d, h))

    def a_wait(b):
        r = pl.ds(pl.multiple_of(b * rows, rows), rows)
        for h in range(2):
            for d in range(1, 4):
                mm = (m + d) % 4
                piece = ab.at[mm, r, pl.ds(h * 128, 128)]
                remote(piece, piece, a_send.at[b, d, h], a_recv.at[b, mm, h], ypeer).wait_recv()

    def partial(b):
        r = pl.ds(pl.multiple_of(b * rows, rows), rows)
        acc = None
        for mm in range(NM):
            term = lax.dot_general(ob[mm], ab[mm, r, :], (((1,), (1,)), ((), ())), preferred_element_type=f32)
            acc = term if acc is None else acc + term
        for hf in range(2):
            pacc[hf] = acc[:, hf * half:(hf + 1) * half]

    def r_copy(side, b, hf, zd):
        return remote(sb.at[b, hf], rb.at[side, b, hf], r_send.at[b, hf], r_recv.at[side, b, hf], at_z(zd))

    def hop(b):
        right = b > z
        side = jnp.where(right, 0, 1)
        target = jnp.where(right, (z + 1) % 4, (z + 3) % 4)
        inner = (right & (z > 0)) | (jnp.logical_not(right) & (z < 3))
        partial(b)
        for hf in range(2):
            @pl.when(inner)
            def _():
                r_copy(side, b, hf, target).wait_recv()
                sb[b, hf] = (pacc[hf] + rb[side, b, hf].astype(f32)).astype(bf16)

            @pl.when(jnp.logical_not(inner))
            def _():
                sb[b, hf] = pacc[hf].astype(bf16)

            r_copy(side, b, hf, target).start()

    def hop_step(k):
        a_wait(order[k])
        hop(order[k])

    def hop_edge(k):
        pl.when(edge)(lambda: hop_step(k))

    def hop_inner(k):
        pl.when(jnp.logical_not(edge))(lambda: hop_step(k))

    steps = {
        "xz": own_z, "xx": own_across, "xc": own_core, "wc": w_cross, "wd": w_direct, "wo": o_half, "wr": w_relay,
        "wy": w_along_y, "xl": from_left, "xr": from_right, "xk": x_cross, "ca": cache, "nm": norm_block,
        "we": w_done, "wm": w_ends, "od": o_done, "cd": c_done, "pq": project_q, "pk": project_kv, "kd": kv_done,
        "tr": angles, "gp": gains, "at": attend, "he": hop_edge, "hi": hop_inner, "hp": hop_step,
    }
    for name, *rest in SCHEDULE:
        steps[name](*rest)

    a_wait(order[3])

    partial(z)

    def add_arrived(side, hf):
        r_copy(side, z, hf, z).wait_recv()
        pacc[hf] += rb[side, z, hf].astype(f32)

    for hf in range(2):
        pl.when(z > 0)(functools.partial(add_arrived, 0, hf))
        pl.when(z < 3)(functools.partial(add_arrived, 1, hf))
        mixed = pacc[hf]
        squares = jnp.sum(mixed * mixed, axis=0, keepdims=True)
        ss[m, :, hf * half:(hf + 1) * half] = jnp.broadcast_to(squares, (8, half))

    def s_copy(d):
        return remote(ss.at[m], ss.at[m], s_send.at[d], s_recv.at[m], {"mp": (m + d) % 4, "seq": s})

    for d in range(1, 4):
        s_copy(d).start()
    for d in range(1, 4):
        mm = (m + d) % 4
        remote(ss.at[mm], ss.at[mm], s_send.at[d], s_recv.at[mm], ypeer).wait_recv()
    squares = (ss[0] + ss[1] + ss[2] + ss[3])[0:1, :]
    scaling = lax.rsqrt(squares / MODEL_WIDTH + epsilon)
    for hf in range(2):
        part = slice(hf * half, (hf + 1) * half)
        out[:, part] = (xb[z, m, hf].astype(f32) + pacc[hf] * scaling[:, part] * g_post[...]).astype(bf16)

    for d in range(1, 4):
        s_copy(d).wait_send()
    for d in range(4):
        for hf in range(2):
            when(z != d, r_copy(0, d, hf, (z + 1) % 4).wait_send)
    for cond, cp in pending:
        when(cond, cp.wait_send)


def fused(
    hidden_in, gain_in, w_query, key_weight, value_weight, gain_query, gain_key, start_pos,
    cached_key_rows, cached_value_rows, w_out, gain_post,
):
    rows, cols = hidden_in.shape
    depth = w_query.shape[0]
    inverse_freq = rope_base ** (-(np.arange(64) * 2.0) / 128)
    freq = jnp.asarray(np.concatenate([inverse_freq, inverse_freq])[None, :], f32)
    hbm = pl.BlockSpec(memory_space=pl.ANY)
    vmem = pl.BlockSpec(memory_space=pltpu.VMEM)
    smem = pl.BlockSpec(memory_space=pltpu.SMEM)
    dma = pltpu.SemaphoreType.DMA
    turned = pl.pallas_call(
        layer_kernel,
        name="layer",
        out_shape=pltpu.VMEM((cols, rows), bf16),
        in_specs=[hbm, vmem, hbm, hbm, hbm, vmem, vmem, smem, vmem, hbm, hbm, hbm, vmem],
        out_specs=vmem,
        scratch_shapes=[
            pltpu.VMEM((1024, 128), f32),
            pltpu.VMEM((1024, 128), f32),
            pltpu.VMEM((4 * cols // 128, 128), f32),
            pltpu.VMEM((cols, 128), f32),
            pltpu.VMEM((4, 4, 2, cols, 128), bf16),
            pltpu.VMEM((4 * rows, 4 * cols), bf16),
            pltpu.VMEM((2, depth, 512), bf16),
            pltpu.VMEM((4, 2 * depth, 512), bf16),
            pltpu.VMEM((256, 512), bf16),
            pltpu.VMEM((4, cols, 256), bf16),
            pltpu.VMEM((3072, 256), bf16),
            pltpu.VMEM((2, 1024, 128), bf16),
            pltpu.VMEM((4, 1024, 256), bf16),
            pltpu.VMEM((2, 4, 2, cols, 128), bf16),
            pltpu.VMEM((4, 2, cols, 128), bf16),
            pltpu.VMEM((4, 8, rows), f32),
            pltpu.VMEM((2, cols, 128), f32),
            dma((10,)), dma((2, 4, 2)), dma((4, 2)), dma((4, 2)), dma((4, 2)), dma((2, 4, 2)), dma((2, 4, 2)),
            dma((4, 3)), dma((2, 3)), dma((2, 3)), dma((4, 3)), dma((4, 3)), dma((4, 3)), dma((4, 2)), dma((2,)), dma((2,)), dma((2,)),
            dma((4,)), dma((4,)), dma((4, 4, 2)), dma((4, 4, 2)), dma((4, 2)), dma((2, 4, 2)), dma((4,)), dma((4,)),
        ],
        compiler_params=pltpu.CompilerParams(
            collective_id=0, has_side_effects=True, vmem_limit_bytes=60 * 1024 * 1024,
        ),
    )(
        hidden_in.T, gain_in.reshape(-1, 128), w_query, key_weight, value_weight,
        gain_query.reshape(1, 128), gain_key.reshape(1, 128), start_pos, freq,
        cached_key_rows, cached_value_rows, w_out.T, gain_post,
    )
    return turned.T


def shifted(x, axis, by):
    peers = lax.axis_size(axis)
    pairs = [(i, i + by) for i in range(peers) if 0 <= i + by < peers]
    return lax.ppermute(x, axis, pairs)


def norm_rows(values, gain):
    return values * lax.rsqrt(jnp.mean(values * values, axis=-1, keepdims=True) + epsilon) * gain


def rotate(tensor, positions):
    half_dim = tensor.shape[-1] // 2
    inverse_freq = rope_base ** (
        -(jnp.arange(half_dim, dtype=jnp.float32) * 2.0) / tensor.shape[-1]
    )
    angles = positions.astype(jnp.float32)[:, None, None] * inverse_freq[None, None, :]
    cosine = jnp.cos(angles)
    sine = jnp.sin(angles)
    first = tensor[..., :half_dim]
    second = tensor[..., half_dim:]
    return jnp.concatenate(
        [first * cosine - second * sine, second * cosine + first * sine], axis=-1
    )


def on_device(
    hidden_in,
    gain_in,
    w_query,
    key_weight,
    value_weight,
    gain_query,
    gain_key,
    start_pos,
    cached_key_rows,
    cached_value_rows,
    w_out,
    gain_post,
):
    n_rows = hidden_in.shape[0]
    head_dim = gain_query.shape[0]
    kv_cols = key_weight.shape[1]
    kv_heads = kv_cols // head_dim
    q_heads = w_query.shape[1] // head_dim
    query_group_count = q_heads // kv_heads
    full_rows = lax.all_gather(hidden_in, "mp", axis=1, tiled=True)
    normed_hidden = norm_rows(full_rows.astype(jnp.float32), gain_in).astype(jnp.bfloat16)

    def add_rows(block_rows):
        return jnp.dot(normed_hidden, block_rows, preferred_element_type=jnp.float32)

    keys_raw = add_rows(lax.all_gather(key_weight, "seq", axis=0, tiled=True))
    values_raw = add_rows(lax.all_gather(value_weight, "seq", axis=0, tiled=True))
    query_matrix = add_rows(lax.all_gather(w_query, "seq", axis=0, tiled=True))
    seq_index = lax.axis_index("seq")
    positions = start_pos[0] + seq_index * n_rows + jnp.arange(n_rows, dtype=jnp.int32)
    query_matrix = (
        rotate(norm_rows(query_matrix.reshape(n_rows, q_heads, head_dim), gain_query), positions)
        * query_scale
    ).astype(jnp.bfloat16)
    fresh_key = rotate(
        norm_rows(keys_raw.reshape(n_rows, kv_heads, head_dim), gain_key), positions
    ).astype(jnp.bfloat16)
    fresh = jnp.stack([fresh_key.reshape(n_rows, kv_cols), values_raw.astype(jnp.bfloat16)])
    reach_shards = (WINDOW_LENGTH + n_rows - 1) // n_rows
    reach_rows = reach_shards * n_rows
    pieces = []
    moving = fresh
    for hop_index in range(reach_shards):
        moving = shifted(moving, "seq", 1)
        pieces.insert(0, moving)
    prior = jnp.concatenate(pieces, axis=1)
    front_pad = reach_rows - WINDOW_LENGTH
    cached = jnp.stack([cached_key_rows, cached_value_rows])
    padded = jnp.concatenate(
        [
            jnp.zeros((2, front_pad, kv_cols), cached.dtype),
            cached,
            jnp.zeros((2, reach_rows, kv_cols), cached.dtype),
        ],
        axis=1,
    )
    cache_start = jnp.minimum(seq_index * n_rows, front_pad + WINDOW_LENGTH)
    from_cache = lax.dynamic_slice_in_dim(padded, cache_start, reach_rows, 1)
    prior_rows = jnp.arange(reach_rows, dtype=jnp.int32)
    use_cache = prior_rows < reach_rows - seq_index * n_rows
    prior = jnp.where(use_cache[None, :, None], from_cache, prior)
    window_kv = jnp.concatenate([prior, fresh], axis=1)
    span_rows = reach_rows + n_rows
    key_heads = window_kv[0].reshape(span_rows, kv_heads, head_dim)
    value_heads = window_kv[1].reshape(span_rows, kv_heads, head_dim)
    query_heads = query_matrix.reshape(n_rows, kv_heads, query_group_count, head_dim)
    scores = jnp.einsum(
        "tkgd,skd->kgts", query_heads, key_heads, preferred_element_type=jnp.float32
    )
    query_index = jnp.arange(n_rows, dtype=jnp.int32)[:, None]
    key_index = jnp.arange(span_rows, dtype=jnp.int32)[None, :]
    visible = (key_index > query_index + reach_rows - WINDOW_LENGTH) & (
        key_index <= query_index + reach_rows
    )
    scores = jnp.where(visible, scores, -jnp.inf)
    row_max = jnp.max(scores, axis=-1, keepdims=True)
    probs = jnp.exp(scores - row_max)
    totals = jnp.sum(probs, axis=-1)
    probs_b = probs.astype(jnp.bfloat16)
    summed = jnp.einsum("kgts,skd->tkgd", probs_b, value_heads, preferred_element_type=jnp.float32)
    summed = summed / jnp.transpose(totals, (2, 0, 1))[..., None]
    attn = summed.reshape(n_rows, q_heads * head_dim).astype(jnp.bfloat16)
    all_heads = lax.all_gather(attn, "mp", axis=1, tiled=True)
    projected = jnp.dot(
        all_heads,
        lax.all_gather(w_out, "seq", axis=0, tiled=True),
        preferred_element_type=jnp.float32,
    )
    squares = lax.psum(jnp.sum(projected * projected, axis=-1), "mp")
    scaling = lax.rsqrt(squares / MODEL_WIDTH + epsilon)
    return (hidden_in.astype(jnp.float32) + projected * scaling[:, None] * gain_post).astype(
        jnp.bfloat16
    )


def solution(mesh):
    in_specs = (
        P("seq", "mp"),
        P(),
        P("seq", "mp"),
        P("seq", "mp"),
        P("seq", "mp"),
        P(),
        P(),
        P(),
        P(None, "mp"),
        P(None, "mp"),
        P("seq", "mp"),
        P("mp"),
    )
    out_specs = P("seq", "mp")
    fits = mesh.shape["mp"] == 4 and mesh.shape["seq"] == 8
    return jax.shard_map(
        fused if fits else on_device, mesh=mesh, in_specs=in_specs, out_specs=out_specs, check_vma=False
    )
```
